32 devices in a mesh: grp: 2 (over x), line: 16 (over z, y, core).
Axes of the slice: x: 2, y: 2, z: 4, core: 2. Of those that a mesh axis runs over, the one named last changes fastest.
Arguments:
- ptdf: bfloat16 [4096, 13824], P('line'), may hold values from -0.109375 to 0.109375
- load: bfloat16 [13824, 256], P('line', 'grp'), parts along dimension 1, may hold values from 0 to 0.29882812
- unit_bus: int32 [1024], replicated, may hold values from 0 to 13823
- min_up: int32 [1024], P('line'), may hold values from 2 to 31
- gen_max: float32 [1024], P('line'), may hold values from 0.5 to 2
- cost_gen: float32 [1024], P('line'), may hold values from 0.5 to 5
- cost_commit: float32 [1024], P('line'), may hold values from 0.5 to 5
- cost_start: float32 [1024], P('line'), may hold values from 0.5 to 5
- init_commit: float32 [1024], P('line'), may hold values from 0 to 1
- line_limit: float32 [4096], P('line'), may hold values from 0.1 to 1
- gen: float32 [1024, 256], P('line', 'grp'), parts along dimension 1, may hold values from 0 to 1
- commit: float32 [1024, 256], P('line', 'grp'), parts along dimension 1, may hold values from 0 to 1
- startup: float32 [1024, 256], P('line', 'grp'), parts along dimension 1, may hold values from 0 to 0.5
- line_dual: float32 [4096, 256], P('line', 'grp'), parts along dimension 1, may hold values from -6 to 6
- balance_dual: float32 [256], P(('grp', 'line')), parts along dimension 0, may hold values from -6 to 6
- cap_dual: float32 [1024, 256], P('line', 'grp'), parts along dimension 1, may hold values from 0 to 1
- start_dual: float32 [1024, 256], P('line', 'grp'), parts along dimension 1, may hold values from 0 to 1
- window_dual: float32 [1024, 256], P('line', 'grp'), parts along dimension 1, may hold values from 0 to 1
Outputs:
- gen_out: float32 [1024, 256], P('line', 'grp'), parts along dimension 1
- commit_out: float32 [1024, 256], P('line', 'grp'), parts along dimension 1
- startup_out: float32 [1024, 256], P('line', 'grp'), parts along dimension 1
- line_dual_out: float32 [4096, 256], P('line', 'grp'), parts along dimension 1
- balance_dual_out: float32 [256], P(('grp', 'line')), parts along dimension 0
- cap_dual_out: float32 [1024, 256], P('line', 'grp'), parts along dimension 1
- start_dual_out: float32 [1024, 256], P('line', 'grp'), parts along dimension 1
- window_dual_out: float32 [1024, 256], P('line', 'grp'), parts along dimension 1
The draws below stay inside these ranges and needn't reach their ends.
There are 2 independent parts, one for each index of `grp`. The reference program is written for one: setup_inputs(seed, part) draws one part's arguments, and reference() takes and returns one part's arrays. A program takes and returns all parts, laid end to end along the dimension named above; an argument that names none is the same for every part. Nothing has to cross between parts.
All inputs are finite; a program needn't handle non-finite values.
Results may differ from the reference program's by a relative error of at most 0.00054.
Values may be sent and summed in bfloat16 or wider, within the bound.
No kernel may reach another device: no remote copies, remote signals or barrier semaphores. Data moves between devices by JAX's collectives and lax.ppermute only.
A program may use at most 64 MiB of HBM per device.

```python
import math
import jax
import jax.numpy as jnp
from jax import lax

B = 13824
T_SIZE = 128
ITERS = 2
LINES = 4096
UNITS = 1024


def with_ends(values, key, low, top_value):
    longest = values.shape.index(max(values.shape))
    spots = []
    for shift in (0, 1):
        where = [jax.random.randint(jax.random.fold_in(key, axis), (), 0, length) for axis, length in enumerate(values.shape)]
        where[longest] = (where[longest] + shift) % values.shape[longest]
        spots.append(tuple(where))
    return values.at[spots[0]].set(low).at[spots[1]].set(top_value)


def raised(array, stream_key, source, target, parts, factor):
    owner, partner = [(jnp.arange(array.shape[axis_at]) // (array.shape[axis_at] // parts)).reshape([-1 if axis == axis_at else 1 for axis in range(array.ndim)]) for axis_at in (source, target)]
    chosen = jax.random.permutation(stream_key, parts)[partner]
    strong = (owner == chosen) | (owner == (partner + parts // 2) % parts)
    return jnp.where(strong, factor * array, array)


def shard_levels(own_key, extent, split, least, largest):
    loudness, own = 1.0, jax.random.fold_in(own_key, 6)
    for position, shards_of in split:
        draws = jnp.exp(jax.random.uniform(jax.random.fold_in(own, position), (shards_of,), jnp.float32, least / len(split), largest / len(split)))
        loudness = loudness * jnp.repeat(draws, extent[position] // shards_of).reshape([-1 if axis == position else 1 for axis in range(len(extent))])
    return loudness


def noise(stream_key, dims, deviation, most, pieces=(), kind=jnp.bfloat16):
    array = jax.random.normal(stream_key, dims, jnp.float32) * deviation
    if len(pieces) > 0:
        array = shard_levels(stream_key, dims, pieces, -0.22, 0.18) * array
    return jnp.clip(array, min=-most, max=most).astype(kind)


def noise_with(key, shape, spread, limit, pieces, heavy, held_as=jnp.bfloat16):
    array = spread * jax.random.normal(key, shape, jnp.float32)
    if pieces:
        array = array * shard_levels(key, shape, pieces, -0.22, 0.18)
    return jnp.clip(raised(array, jax.random.fold_in(key, 3), *heavy), -limit, limit).astype(held_as)


def setup_inputs(seed: int = 0, part: int = 0) -> dict:
    streams_of = jax.random.split(jax.random.key(seed), 19)
    part_keys = jax.random.split(jax.random.fold_in(streams_of[18], part), 19)
    ptdf = noise(streams_of[0], (LINES, B), (B // 4) ** -0.5, 0.109375, ((0, 16),))
    load = jnp.clip(0.29882812 * jax.random.uniform(part_keys[1], (B, T_SIZE), jnp.float32) ** shard_levels(part_keys[1], (B, T_SIZE), ((0, 16),), -0.2, 0.2), 0.0, 0.29882812).astype(jnp.bfloat16)
    unit_bus = with_ends(jax.random.randint(streams_of[2], (UNITS,), 0, B), jax.random.fold_in(streams_of[2], 1), 0, B - 1).astype(jnp.int32)
    min_up = with_ends(jax.random.randint(streams_of[3], (UNITS,), 2, T_SIZE // 4), jax.random.fold_in(streams_of[3], 1), 2, (T_SIZE // 4) - 1).astype(jnp.int32)
    gen_max = jnp.clip(jnp.exp(math.log(2.0) - 1.3862944 * jax.random.uniform(streams_of[4], (UNITS,), jnp.float32) ** shard_levels(streams_of[4], (UNITS,), ((0, 16),), -0.2, 0.2)), 0.5, 2.0)
    cost_gen = jnp.clip(jnp.exp(math.log(5.0) - 2.3025851 * jax.random.uniform(streams_of[5], (UNITS,), jnp.float32) ** shard_levels(streams_of[5], (UNITS,), ((0, 16),), -0.2, 0.2)), 0.5, 5.0)
    cost_commit = jnp.clip(jnp.exp(math.log(5.0) - 2.3025851 * jax.random.uniform(streams_of[6], (UNITS,), jnp.float32) ** shard_levels(streams_of[6], (UNITS,), ((0, 16),), -0.2, 0.2)), 0.5, 5.0)
    cost_start = jnp.clip(jnp.exp(math.log(5.0) - 2.3025851 * jax.random.uniform(streams_of[7], (UNITS,), jnp.float32) ** shard_levels(streams_of[7], (UNITS,), ((0, 16),), -0.2, 0.2)), 0.5, 5.0)
    init_commit = jnp.clip(1.0 * jax.random.uniform(streams_of[8], (UNITS,), jnp.float32) ** shard_levels(streams_of[8], (UNITS,), ((0, 16),), -0.2, 0.2), 0.0, 1.0)
    line_limit = jnp.clip(0.1 + 0.9 * jax.random.uniform(streams_of[9], (LINES,), jnp.float32) ** shard_levels(streams_of[9], (LINES,), ((0, 16),), -0.2, 0.2), 0.1, 1.0)
    gen = jnp.clip(1.0 * jax.random.uniform(part_keys[10], (UNITS, T_SIZE), jnp.float32) ** shard_levels(part_keys[10], (UNITS, T_SIZE), ((0, 16),), -0.2, 0.2), 0.0, 1.0)
    commit = jnp.clip(1.0 * jax.random.uniform(part_keys[11], (UNITS, T_SIZE), jnp.float32) ** shard_levels(part_keys[11], (UNITS, T_SIZE), ((0, 16),), -0.2, 0.2), 0.0, 1.0)
    startup = jnp.clip(0.5 * jax.random.uniform(part_keys[12], (UNITS, T_SIZE), jnp.float32) ** shard_levels(part_keys[12], (UNITS, T_SIZE), ((0, 16),), -0.2, 0.2), 0.0, 0.5)
    line_dual = noise_with(part_keys[13], (LINES, T_SIZE), 1.0, 6.0, ((0, 16),), (0, 1, 16, 2.0), jnp.float32)
    balance_dual = noise(part_keys[14], (T_SIZE,), 1.0, 6.0, ((0, 16),), jnp.float32)
    cap_dual = jnp.clip(1.0 * jax.random.uniform(part_keys[15], (UNITS, T_SIZE), jnp.float32) ** shard_levels(part_keys[15], (UNITS, T_SIZE), ((0, 16),), -0.2, 0.2), 0.0, 1.0)
    start_dual = jnp.clip(1.0 * jax.random.uniform(part_keys[16], (UNITS, T_SIZE), jnp.float32) ** shard_levels(part_keys[16], (UNITS, T_SIZE), ((0, 16),), -0.2, 0.2), 0.0, 1.0)
    window_dual = jnp.clip(1.0 * jax.random.uniform(part_keys[17], (UNITS, T_SIZE), jnp.float32) ** shard_levels(part_keys[17], (UNITS, T_SIZE), ((0, 16),), -0.2, 0.2), 0.0, 1.0)
    return {"ptdf": ptdf, "load": load, "unit_bus": unit_bus, "min_up": min_up, "gen_max": gen_max, "cost_gen": cost_gen, "cost_commit": cost_commit, "cost_start": cost_start, "init_commit": init_commit, "line_limit": line_limit, "gen": gen, "commit": commit, "startup": startup, "line_dual": line_dual, "balance_dual": balance_dual, "cap_dual": cap_dual, "start_dual": start_dual, "window_dual": window_dual}


TAU_STEP = 0.05
SIGMA_STEP = 0.5


def prefix_sums(values):
    zeros_column = jnp.zeros((values.shape[0], 1), jnp.float32)
    return jnp.concatenate([zeros_column, jnp.cumsum(values, axis=1)], axis=1)


def window_indices(min_up, periods):
    positions = jnp.broadcast_to(jnp.arange(periods, dtype=jnp.int32)[None, :], (min_up.shape[0], periods))
    spans = min_up.astype(jnp.int32)[:, None]
    lower_end = jnp.maximum(positions + 1 - spans, 0).astype(jnp.int32)
    upper_end = jnp.minimum(positions + spans, periods).astype(jnp.int32)
    return positions, lower_end, upper_end


def window_forward(values, positions, lower_end):
    sums = prefix_sums(values)
    return jnp.take_along_axis(sums, positions + 1, axis=1) - jnp.take_along_axis(sums, lower_end, axis=1)


def window_backward(values, positions, upper_end):
    sums = prefix_sums(values)
    return jnp.take_along_axis(sums, upper_end, axis=1) - jnp.take_along_axis(sums, positions, axis=1)


def primal_update(gen, commit, startup, adjoint_gen, start_dual, window_dual, gen_max, cost_gen, cost_commit, cost_start, cap_dual, positions, upper_end):
    zeros_column = jnp.zeros((start_dual.shape[0], 1), jnp.float32)
    later_start = jnp.concatenate([start_dual[:, 1:], zeros_column], axis=1)
    grad_gen = cost_gen[:, None] + adjoint_gen
    grad_commit = cost_commit[:, None] - gen_max[:, None] * cap_dual + start_dual - later_start - window_dual
    grad_start = cost_start[:, None] - start_dual + window_backward(window_dual, positions, upper_end)
    new_gen = jnp.clip(gen - TAU_STEP * grad_gen, 0.0, gen_max[:, None])
    new_commit = jnp.clip(commit - TAU_STEP * grad_commit, 0.0, 1.0)
    new_start = jnp.clip(startup - TAU_STEP * grad_start, 0.0, 1.0)
    return new_gen, new_commit, new_start


def unit_dual_update(bar_gen, bar_commit, bar_start, cap_dual, start_dual, window_dual, gen_max, init_commit, positions, lower_end):
    new_cap = jnp.maximum(0.0, cap_dual + SIGMA_STEP * (bar_gen - gen_max[:, None] * bar_commit))
    previous = jnp.concatenate([init_commit[:, None], bar_commit[:, :-1]], axis=1)
    new_start = jnp.maximum(0.0, start_dual + SIGMA_STEP * (bar_commit - previous - bar_start))
    new_window = jnp.maximum(0.0, window_dual + SIGMA_STEP * (window_forward(bar_start, positions, lower_end) - bar_commit))
    return new_cap, new_start, new_window


def line_update(line_dual, flows, line_limit):
    shifted = line_dual + SIGMA_STEP * flows
    limits = line_limit[:, None]
    return shifted - SIGMA_STEP * jnp.clip(shifted / SIGMA_STEP, -limits, limits)


def reference(ptdf, load, unit_bus, min_up, gen_max, cost_gen, cost_commit, cost_start, init_commit, line_limit, gen, commit, startup, line_dual, balance_dual, cap_dual, start_dual, window_dual):
    highest = lax.Precision.HIGHEST
    unit_cols = jnp.take(ptdf, unit_bus, axis=1).astype(jnp.float32)
    load_flow = jnp.dot(ptdf.astype(jnp.float32), load.astype(jnp.float32), precision=highest)
    demand = jnp.sum(load.astype(jnp.float32), axis=0)
    unit_count = unit_cols.shape[1]
    positions, lower_end, upper_end = window_indices(min_up, gen.shape[1])
    for step in range(ITERS):
        dual_half = lax.optimization_barrier(line_dual.astype(jnp.bfloat16))
        weighted = jnp.dot(unit_cols.T, dual_half.astype(jnp.float32), precision=highest)
        adjoint_gen = weighted + balance_dual[None, :] + cap_dual
        new_gen, new_commit, new_start = primal_update(gen, commit, startup, adjoint_gen, start_dual, window_dual, gen_max, cost_gen, cost_commit, cost_start, cap_dual, positions, upper_end)
        bar_gen = 2.0 * new_gen - gen
        bar_commit = 2.0 * new_commit - commit
        bar_start = 2.0 * new_start - startup
        bar_half = lax.optimization_barrier(bar_gen.astype(jnp.bfloat16))
        bar_wide = bar_half.astype(jnp.float32)
        flows = jnp.dot(unit_cols, bar_wide, precision=highest) - load_flow
        totals = jnp.sum(bar_wide, axis=0)
        line_dual = line_update(line_dual, flows, line_limit)
        balance_dual = balance_dual + (totals - demand) / unit_count
        cap_dual, start_dual, window_dual = unit_dual_update(bar_gen, bar_commit, bar_start, cap_dual, start_dual, window_dual, gen_max, init_commit, positions, lower_end)
        gen, commit, startup = new_gen, new_commit, new_start
    return (gen, commit, startup, line_dual, balance_dual, cap_dual, start_dual, window_dual)
```

```python
import functools

import jax
import jax.numpy as jnp
from jax import lax
from jax.experimental import pallas as pl
from jax.experimental.pallas import tpu as pltpu
from jax.sharding import PartitionSpec as P

ITERS = 2
TAU = 0.05
SIGMA = 0.5
SPAN_BITS = 5

F32 = jnp.float32
BF16 = jnp.bfloat16
VMEM = pl.BlockSpec(memory_space=pltpu.VMEM)


def shift_right(values, amount):
    lanes = lax.broadcasted_iota(jnp.int32, values.shape, 1)
    return jnp.where(lanes >= amount, pltpu.roll(values, amount, 1), 0.0)


def shift_left(values, amount):
    periods = values.shape[1]
    lanes = lax.broadcasted_iota(jnp.int32, values.shape, 1)
    return jnp.where(lanes < periods - amount, pltpu.roll(values, periods - amount, 1), 0.0)


def window_sum(values, spans, shift):
    block = values
    total = jnp.zeros_like(values)
    for bit in range(SPAN_BITS):
        chosen = (lax.shift_right_logical(spans, bit) & 1) == 1
        total = jnp.where(chosen, block + shift(total, 1 << bit), total)
        if bit + 1 < SPAN_BITS:
            block = block + shift(block, 1 << bit)
    return total


def ahead_kernel(par, spans_ref, commit, startup, cap, start, window,
                 commit1, bar_commit1, start1, window1, startup2, grad2, bar_start2, reach2):
    gen_max, cost_commit, cost_start, init = (par[:, i:i + 1] for i in (0, 2, 3, 4))
    spans = jnp.broadcast_to(spans_ref[...], commit.shape)
    lanes = lax.broadcasted_iota(jnp.int32, commit.shape, 1)
    c0, s0, sd0, wd0 = commit[...], startup[...], start[...], window[...]
    grad_c = cost_commit - gen_max * cap[...] + sd0 - shift_left(sd0, 1) - wd0
    grad_s = cost_start - sd0 + window_sum(wd0, spans, shift_left)
    c1 = jnp.clip(c0 - TAU * grad_c, 0.0, 1.0)
    s1 = jnp.clip(s0 - TAU * grad_s, 0.0, 1.0)
    bc1 = 2.0 * c1 - c0
    bs1 = 2.0 * s1 - s0
    before = jnp.where(lanes == 0, init, pltpu.roll(bc1, 1, 1))
    sd1 = jnp.maximum(0.0, sd0 + SIGMA * (bc1 - before - bs1))
    wd1 = jnp.maximum(0.0, wd0 + SIGMA * (window_sum(bs1, spans, shift_right) - bc1))
    grad_s2 = cost_start - sd1 + window_sum(wd1, spans, shift_left)
    s2 = jnp.clip(s1 - TAU * grad_s2, 0.0, 1.0)
    bs2 = 2.0 * s2 - s1
    commit1[...] = c1
    bar_commit1[...] = bc1
    start1[...] = sd1
    window1[...] = wd1
    startup2[...] = s2
    grad2[...] = cost_commit + sd1 - shift_left(sd1, 1) - wd1
    bar_start2[...] = bs2
    reach2[...] = window_sum(bs2, spans, shift_right)


def columns_kernel(bus, ptdf, cols_t, cols, acc):
    step = pl.program_id(0)
    depth = ptdf.shape[1]
    here = bus[...] - step * depth
    hot = (lax.broadcasted_iota(jnp.int32, (bus.shape[0], depth), 1) == here).astype(F32).astype(BF16)
    part = lax.dot_general(hot, ptdf[...], (((1,), (1,)), ((), ())), preferred_element_type=F32)

    @pl.when(step == 0)
    def _():
        acc[...] = part

    @pl.when(step > 0)
    def _():
        acc[...] += part

    @pl.when(step == pl.num_programs(0) - 1)
    def _():
        total = acc[...]
        cols_t[...] = total.astype(BF16)
        cols[...] = total.T.astype(BF16)


def load_kernel(ptdf, load, flow, demand):
    step = pl.program_id(0)
    block = load[...]
    part = jnp.dot(ptdf[...], block, preferred_element_type=F32)
    rows = jnp.sum(block.astype(F32).reshape(-1, 8, block.shape[1]), axis=0)

    @pl.when(step == 0)
    def _():
        flow[...] = part
        demand[...] = rows

    @pl.when(step > 0)
    def _():
        flow[...] += part
        demand[...] += rows


def adjoint_kernel(cols_t, line_dual, balance, part):
    part[...] = (
        jnp.dot(cols_t[...], line_dual[...].astype(BF16), preferred_element_type=F32) + balance[...]
    )


def gen_step(parts, gen, cap, par):
    gen_max, cost_gen = par[:, 0:1], par[:, 1:2]
    weighted = parts[0]
    for i in range(1, parts.shape[0]):
        weighted = weighted + parts[i]
    g0 = gen[...]
    g1 = jnp.clip(g0 - TAU * (cost_gen + (weighted + cap[...])), 0.0, gen_max)
    return g1, 2.0 * g1 - g0


def gen1_kernel(parts, gen, cap, bar_commit, par, spread, gen_out, cap_out):
    g1, bar = gen_step(parts, gen, cap, par)
    half = bar.astype(BF16)
    for i in range(spread.shape[0]):
        spread[i] = half
    gen_out[...] = g1
    cap_out[...] = jnp.maximum(0.0, cap[...] + SIGMA * (bar - par[:, 0:1] * bar_commit[...]))


def gen2_kernel(parts, gen, cap, par, commit, start, window, grad, bar_start, reach,
                spread, gen_out, commit_out, cap_out, start_out, window_out):
    g2, bar = gen_step(parts, gen, cap, par)
    half = bar.astype(BF16)
    for i in range(spread.shape[0]):
        spread[i] = half
    gen_out[...] = g2
    gen_max, init = par[:, 0:1], par[:, 4:5]
    lanes = lax.broadcasted_iota(jnp.int32, gen.shape, 1)
    cap1, c1 = cap[...], commit[...]
    c2 = jnp.clip(c1 - TAU * (grad[...] - gen_max * cap1), 0.0, 1.0)
    bc2 = 2.0 * c2 - c1
    before = jnp.where(lanes == 0, init, pltpu.roll(bc2, 1, 1))
    commit_out[...] = c2
    cap_out[...] = jnp.maximum(0.0, cap1 + SIGMA * (bar - gen_max * bc2))
    start_out[...] = jnp.maximum(0.0, start[...] + SIGMA * (bc2 - before - bar_start[...]))
    window_out[...] = jnp.maximum(0.0, window[...] + SIGMA * (reach[...] - bc2))


def line_step(cols, bars, flow, dual, limit):
    flows = jnp.dot(cols[...], bars[...], preferred_element_type=F32) - flow[...]
    shifted = dual[...] + SIGMA * flows
    bound = limit[...]
    return shifted - SIGMA * jnp.clip(shifted / SIGMA, -bound, bound)


def balance_step(bars, demand, balance):
    totals = jnp.sum(bars[...].astype(F32).reshape(-1, 8, bars.shape[1]), axis=0)
    change = jnp.sum(totals - demand[...], axis=0, keepdims=True)
    return balance[...] + change / bars.shape[0]


def line1_kernel(cols, cols_t, bars, flow, demand, dual, limit, balance, own,
                 part, dual_out, balance_out):
    new = line_step(cols, bars, flow, dual, limit)
    dual_out[...] = new
    moved = balance_step(bars, demand, balance) * own[...]
    balance_out[...] = moved
    part[...] = jnp.dot(cols_t[...], new.astype(BF16), preferred_element_type=F32) + moved


def line2_kernel(cols, bars, flow, demand, dual, limit, balance, dual_out, balance_out):
    dual_out[...] = line_step(cols, bars, flow, dual, limit)
    balance_out[...] = balance_step(bars, demand, balance)


def call(kernel, outs, *args, cost=None):
    shapes = [jax.ShapeDtypeStruct(shape, dtype) for shape, dtype in outs]
    return pl.pallas_call(
        kernel,
        out_shape=shapes,
        in_specs=[VMEM] * len(args),
        out_specs=[VMEM] * len(shapes),
        cost_estimate=cost,
    )(*args)


def block_depth(buses, most):
    return max(d for d in range(128, most + 1, 128) if buses % d == 0)


def on_device(
    ptdf, load, unit_bus, min_up, gen_max, cost_gen, cost_commit, cost_start, init_commit,
    line_limit, gen, commit, startup, line_dual, balance_dual, cap_dual, start_dual, window_dual,
):
    unit_dev, periods = gen.shape
    lines, buses = ptdf.shape
    units = unit_bus.shape[0]
    devices = lax.axis_size("line")
    period_dev = periods // devices
    me = lax.axis_index("line")
    every_load = lax.all_gather(load, "line", axis=0, tiled=True)

    par = jnp.stack(
        [gen_max, cost_gen, cost_commit, cost_start, init_commit, gen_max, gen_max, gen_max], axis=1
    )
    limit = line_limit[:, None]
    places = lax.broadcasted_iota(jnp.int32, (1, periods), 1)
    own = (places // period_dev == me).astype(F32)
    balance = jnp.tile(balance_dual, devices)[None, :] * own

    depth = block_depth(buses, 1536)
    cols_t, cols = pl.pallas_call(
        columns_kernel,
        grid=(buses // depth,),
        out_shape=[
            jax.ShapeDtypeStruct((units, lines), BF16),
            jax.ShapeDtypeStruct((lines, units), BF16),
        ],
        in_specs=[
            pl.BlockSpec((units, 1), lambda k: (0, 0)),
            pl.BlockSpec((lines, depth), lambda k: (0, k)),
        ],
        out_specs=[
            pl.BlockSpec((units, lines), lambda k: (0, 0)),
            pl.BlockSpec((lines, units), lambda k: (0, 0)),
        ],
        scratch_shapes=[pltpu.VMEM((units, lines), F32)],
    )(unit_bus[:, None], ptdf)

    square = (unit_dev, periods)
    parts = call(adjoint_kernel, [((units, periods), F32)], cols_t, line_dual, balance)[0]
    parts = lax.all_to_all(parts, "line", 0, 0, tiled=True).reshape(devices, *square)
    commit1, bar_commit1, start1, window1, startup2, grad2, bar_start2, reach2 = call(
        ahead_kernel, [(square, F32)] * 8, par, min_up[:, None], commit, startup, cap_dual,
        start_dual, window_dual,
    )
    spread, gen1, cap1 = call(
        gen1_kernel, [((devices, *square), BF16)] + [(square, F32)] * 2,
        parts, gen, cap_dual, bar_commit1, par,
    )
    bars = lax.all_to_all(spread, "line", 0, 0).reshape(units, periods)

    depth = block_depth(buses, 1536)
    flow, demand = pl.pallas_call(
        load_kernel,
        grid=(buses // depth,),
        out_shape=[
            jax.ShapeDtypeStruct((lines, periods), F32),
            jax.ShapeDtypeStruct((8, periods), F32),
        ],
        in_specs=[
            pl.BlockSpec((lines, depth), lambda k: (0, k)),
            pl.BlockSpec((depth, periods), lambda k: (k, 0)),
        ],
        out_specs=[
            pl.BlockSpec((lines, periods), lambda k: (0, 0)),
            pl.BlockSpec((8, periods), lambda k: (0, 0)),
        ],
    )(ptdf, every_load)

    parts, dual1, balance1 = call(
        line1_kernel,
        [((units, periods), F32), ((lines, periods), F32), ((1, periods), F32)],
        cols, cols_t, bars, flow, demand, line_dual, limit, balance, own,
    )
    parts = lax.all_to_all(parts, "line", 0, 0, tiled=True).reshape(devices, *square)
    spread, gen2, commit2, cap2, start2, window2 = call(
        gen2_kernel, [((devices, *square), BF16)] + [(square, F32)] * 5,
        parts, gen1, cap1, par, commit1, start1, window1, grad2, bar_start2, reach2,
    )
    bars = lax.all_to_all(spread, "line", 0, 0).reshape(units, periods)
    dual2, balance2 = call(
        line2_kernel, [((lines, periods), F32), ((1, periods), F32)],
        cols, bars, flow, demand, dual1, limit, balance1,
    )
    balance_out = lax.dynamic_slice_in_dim(balance2[0], me * period_dev, period_dev)
    return (gen2, commit2, startup2, dual2, balance_out, cap2, start2, window2)


def solution(mesh):
    wide = P("line", "grp")
    unit = P("line")
    both = P(("grp", "line"))
    in_specs = (
        P("line", None), wide, P(), unit, unit, unit, unit, unit, unit, unit,
        wide, wide, wide, wide, both, wide, wide, wide,
    )
    out_specs = (wide, wide, wide, wide, both, wide, wide, wide)
    return jax.shard_map(
        on_device, mesh=mesh, in_specs=in_specs, out_specs=out_specs, check_vma=False
    )
```

```python
import jax
import jax.numpy as jnp
from jax import lax
from jax.experimental import pallas as pl
from jax.experimental.pallas import tpu as pltpu
from jax.sharding import Mesh, PartitionSpec as P

ITERS = 2
TAU = 0.05
SIGMA = 0.5
SPAN_BITS = 5

F32 = jnp.float32
BF16 = jnp.bfloat16
LINE = ("chip", "core")
SWAP = [(0, 1), (1, 0)]
VMEM = pl.BlockSpec(memory_space=pltpu.VMEM)
SMEM = pl.BlockSpec(memory_space=pltpu.SMEM)

LIMIT, GEN_MAX, COST_GEN, BALANCE = 0, 1, 2, 3


def shift_right(values, amount):
    lanes = lax.broadcasted_iota(jnp.int32, values.shape, 1)
    return jnp.where(lanes >= amount, pltpu.roll(values, amount, 1), 0.0)


def shift_left(values, amount):
    periods = values.shape[1]
    lanes = lax.broadcasted_iota(jnp.int32, values.shape, 1)
    return jnp.where(lanes < periods - amount, pltpu.roll(values, periods - amount, 1), 0.0)


def window_sum(values, spans, shift):
    block = values
    total = jnp.zeros_like(values)
    for bit in range(SPAN_BITS):
        chosen = (lax.shift_right_logical(spans, bit) & 1) == 1
        total = jnp.where(chosen, block + shift(total, 1 << bit), total)
        if bit + 1 < SPAN_BITS:
            block = block + shift(block, 1 << bit)
    return total


def diagonal(rows, columns):
    shape = (rows, columns)
    return lax.broadcasted_iota(jnp.int32, shape, 0) == lax.broadcasted_iota(jnp.int32, shape, 1)


def to_column(row):
    size = row.shape[1]
    return jnp.sum(jnp.where(diagonal(size, size), row, 0.0), axis=1, keepdims=True)


def to_row(column):
    size = column.shape[0]
    return jnp.sum(jnp.where(diagonal(size, size), column, 0.0), axis=0, keepdims=True)


def half_of(values, core):
    half = values.shape[0] // 2
    return jnp.where(core == 0, values[:half], values[half:])


def by_core(mine, other, core):
    return jnp.where(
        core == 0,
        jnp.concatenate([mine, other], axis=1),
        jnp.concatenate([other, mine], axis=1),
    )


def rows_kernel(place, limit, gen_max, cost_gen, balance, out):
    core, chip = place[0], place[1]
    wide = out.shape[1]

    def put(row):
        return jnp.concatenate([row, jnp.zeros((1, wide - row.shape[1]), F32)], axis=1)

    units, periods = gen_max.shape[1], balance.shape[1]
    out[...] = jnp.zeros_like(out)
    out[LIMIT:LIMIT + 1] = limit[...]
    out[GEN_MAX:GEN_MAX + 1] = pltpu.roll(put(gen_max[...]), core * units, 1)
    out[COST_GEN:COST_GEN + 1] = pltpu.roll(put(cost_gen[...]), core * units, 1)
    out[BALANCE:BALANCE + 1] = pltpu.roll(put(balance[...]), (2 * chip + core) * periods, 1)


def ahead_kernel(par, spans_ref, gen, commit, startup, cap, start, window,
                 pack, commit1, start1, window1, startup2, grad2, bar_start2, reach2):
    gen_max, cost_commit, cost_start, init = (par[:, i:i + 1] for i in range(4))
    spans = jnp.broadcast_to(spans_ref[...], commit.shape)
    lanes = lax.broadcasted_iota(jnp.int32, commit.shape, 1)
    c0, s0, sd0, wd0 = commit[...], startup[...], start[...], window[...]
    grad_c = cost_commit - gen_max * cap[...] + sd0 - shift_left(sd0, 1) - wd0
    grad_s = cost_start - sd0 + window_sum(wd0, spans, shift_left)
    c1 = jnp.clip(c0 - TAU * grad_c, 0.0, 1.0)
    s1 = jnp.clip(s0 - TAU * grad_s, 0.0, 1.0)
    bc1 = 2.0 * c1 - c0
    bs1 = 2.0 * s1 - s0
    before = jnp.where(lanes == 0, init, pltpu.roll(bc1, 1, 1))
    sd1 = jnp.maximum(0.0, sd0 + SIGMA * (bc1 - before - bs1))
    wd1 = jnp.maximum(0.0, wd0 + SIGMA * (window_sum(bs1, spans, shift_right) - bc1))
    grad_s2 = cost_start - sd1 + window_sum(wd1, spans, shift_left)
    s2 = jnp.clip(s1 - TAU * grad_s2, 0.0, 1.0)
    bs2 = 2.0 * s2 - s1
    units = gen.shape[0]
    pack[0:units] = gen[...]
    pack[units:2 * units] = cap[...]
    pack[2 * units:3 * units] = bc1
    commit1[...] = c1
    start1[...] = sd1
    window1[...] = wd1
    startup2[...] = s2
    grad2[...] = cost_commit + sd1 - shift_left(sd1, 1) - wd1
    bar_start2[...] = bs2
    reach2[...] = window_sum(bs2, spans, shift_right)


def columns_kernel(bus, ptdf, cols, acc):
    step = pl.program_id(0)
    depth = ptdf.shape[1]
    here = bus[...] - step * depth
    places = lax.broadcasted_iota(jnp.int32, (depth, bus.shape[1]), 0)
    hot = jnp.where(places == here, 1.0, 0.0).astype(BF16)
    part = jnp.dot(ptdf[...], hot, preferred_element_type=F32)

    @pl.when(step == 0)
    def _():
        acc[...] = part

    @pl.when(step > 0)
    def _():
        acc[...] += part

    @pl.when(step == pl.num_programs(0) - 1)
    def _():
        cols[...] = acc[...].astype(BF16)


def put_parts(part, dual, cols_m, cols_o, balance):
    lines = cols_m.shape[0]
    half = dual.astype(BF16)
    total = jnp.dot(half[:, :lines], cols_m[...], preferred_element_type=F32)
    total += jnp.dot(half[:, lines:], cols_o[...], preferred_element_type=F32)
    total += balance
    wide = part.shape[2]
    for i in range(part.shape[0]):
        part[i] = total[:, i * wide:(i + 1) * wide]


def adjoint_kernel(place, cols_m, cols_o, dual_m, dual_o, rows_m, rows_o, part, dual_t, balance):
    core = place[0]
    periods = dual_m.shape[1]
    dual = jnp.concatenate([half_of(dual_m[...].T, core), half_of(dual_o[...].T, core)], axis=1)
    dual_t[...] = dual
    row = rows_m[BALANCE:BALANCE + 1, :periods] + rows_o[BALANCE:BALANCE + 1, :periods]
    column = half_of(to_column(row), core)
    balance[...] = column
    put_parts(part, dual, cols_m, cols_o, column)


def gen_step(parts, gen, cap, rows_m, rows_o):
    wide = gen.shape[1]

    def row(i):
        return rows_m[i:i + 1, :wide] + rows_o[i:i + 1, :wide]

    weighted = parts[0]
    for i in range(1, parts.shape[0]):
        weighted = weighted + parts[i]
    gen_max = row(GEN_MAX)
    g1 = jnp.clip(gen - TAU * (row(COST_GEN) + (weighted + cap)), 0.0, gen_max)
    return g1, 2.0 * g1 - gen, gen_max


def gen1_kernel(place, parts, pack_m, pack_o, rows_m, rows_o, spread, state):
    core = place[0]
    units = pack_m.shape[0] // 3

    def turned(i):
        rows = slice(i * units, (i + 1) * units)
        return by_core(half_of(pack_m[rows].T, core), half_of(pack_o[rows].T, core), core)

    cap = turned(1)
    g1, bar, gen_max = gen_step(parts, turned(0), cap, rows_m, rows_o)
    half = bar.astype(BF16)
    for i in range(spread.shape[0]):
        spread[i] = half
    state[0] = g1
    state[1] = jnp.maximum(0.0, cap + SIGMA * (bar - gen_max * turned(2)))


def gen2_kernel(parts, state, rows_m, rows_o, spread, gen_out):
    g2, bar, _ = gen_step(parts, state[0], state[1], rows_m, rows_o)
    half = bar.astype(BF16)
    for i in range(spread.shape[0]):
        spread[i] = half
    gen_out[...] = g2


def own_units(mine, other, core):
    units = mine.shape[1] // 2
    here, there = mine.T, other.T
    here = jnp.where(core == 0, here[:units], here[units:])
    there = jnp.where(core == 0, there[:units], there[units:])
    return by_core(here, there, core)


def late_kernel(place, par, state_m, state_o, commit, start, window, grad, bar_start, reach,
                gen1, cap1, bar_commit, commit_out, start_out, window_out):
    core = place[0]
    gen_max, init = par[:, 0:1], par[:, 3:4]
    cap = own_units(state_m[1], state_o[1], core)
    gen1[...] = own_units(state_m[0], state_o[0], core)
    cap1[...] = cap
    lanes = lax.broadcasted_iota(jnp.int32, commit.shape, 1)
    c1 = commit[...]
    c2 = jnp.clip(c1 - TAU * (grad[...] - gen_max * cap), 0.0, 1.0)
    bc2 = 2.0 * c2 - c1
    before = jnp.where(lanes == 0, init, pltpu.roll(bc2, 1, 1))
    commit_out[...] = c2
    bar_commit[...] = bc2
    start_out[...] = jnp.maximum(0.0, start[...] + SIGMA * (bc2 - before - bar_start[...]))
    window_out[...] = jnp.maximum(0.0, window[...] + SIGMA * (reach[...] - bc2))


def units_kernel(place, par, gen_m, gen_o, gen1, cap1, bar_commit, gen_out, cap_out):
    g2 = own_units(gen_m[...], gen_o[...], place[0])
    gen_out[...] = g2
    bar = 2.0 * g2 - gen1[...]
    cap_out[...] = jnp.maximum(0.0, cap1[...] + SIGMA * (bar - par[:, 0:1] * bar_commit[...]))


def load_kernel(place, ptdf, load, keep, send, demand, flow):
    step = pl.program_id(0)
    block = load[...]
    part = jnp.dot(ptdf[...], block, preferred_element_type=F32)
    rows = jnp.sum(block.astype(F32).reshape(-1, 8, block.shape[1]), axis=0)

    @pl.when(step == 0)
    def _():
        flow[...] = part
        demand[...] = rows

    @pl.when(step > 0)
    def _():
        flow[...] += part
        demand[...] += rows

    @pl.when(step == pl.num_programs(0) - 1)
    def _():
        turned = flow[...].T
        keep[...] = half_of(turned, place[0])
        send[...] = half_of(turned, 1 - place[0])


def line_step(bars, cols_m, cols_o, flow_m, flow_o, dual, rows_m, rows_o, held):
    wide = bars.shape[2]
    for i in range(bars.shape[0]):
        held[:, i * wide:(i + 1) * wide] = bars[i]
    bar = held[...]
    turn = (((1,), (1,)), ((), ()))
    mine = lax.dot_general(bar, cols_m[...], turn, preferred_element_type=F32) - flow_m[...]
    other = lax.dot_general(bar, cols_o[...], turn, preferred_element_type=F32) - flow_o[...]
    flows = jnp.concatenate([mine, other], axis=1)
    bound = jnp.concatenate([rows_m[LIMIT:LIMIT + 1], rows_o[LIMIT:LIMIT + 1]], axis=1)
    shifted = dual[...] + SIGMA * flows
    new = shifted - SIGMA * jnp.clip(shifted / SIGMA, -bound, bound)
    totals = jnp.sum(bar.astype(F32), axis=1, keepdims=True)
    return new, totals


def balance_step(place, totals, demand, balance, units):
    wanted = to_column(jnp.sum(demand[...], axis=0, keepdims=True))
    change = (totals - half_of(wanted, place[0])) / units
    return balance[...] + change


def line1_kernel(place, bars, cols_m, cols_o, flow_m, flow_o, dual, rows_m, rows_o, demand,
                 balance, part, dual_out, balance_out, held):
    new, totals = line_step(bars, cols_m, cols_o, flow_m, flow_o, dual, rows_m, rows_o, held)
    dual_out[...] = new
    periods = totals.shape[0]
    own = 2 * periods // part.shape[0]
    rows = lax.broadcasted_iota(jnp.int32, totals.shape, 0) + place[0] * periods
    held_here = (rows >= place[1] * own) & (rows < (place[1] + 1) * own)
    moved = balance_step(place, totals, demand, balance, cols_m.shape[1])
    moved = jnp.where(held_here, moved, 0.0)
    balance_out[...] = moved
    put_parts(part, new, cols_m, cols_o, moved)


def line2_kernel(place, bars, cols_m, cols_o, flow_m, flow_o, dual, rows_m, rows_o, demand,
                 balance, keep, send, held):
    new, totals = line_step(bars, cols_m, cols_o, flow_m, flow_o, dual, rows_m, rows_o, held)
    lines, periods = cols_m.shape[0], totals.shape[0]
    moved = to_row(balance_step(place, totals, demand, balance, cols_m.shape[1]))
    moved = jnp.concatenate([moved, jnp.zeros((1, lines - periods), F32)], axis=1)
    extra = jnp.broadcast_to(moved, (8, lines))
    keep[0:periods] = new[:, :lines]
    keep[periods:] = extra
    send[0:periods] = new[:, lines:]
    send[periods:] = extra


def last_kernel(place, mine, other, dual_out, balance_out):
    core, chip = place[0], place[1]
    half = dual_out.shape[1] // 2
    dual_out[...] = by_core(mine[0:half].T, other[0:half].T, core)
    own = balance_out.shape[1]
    first = (2 * chip + core) * own
    side = first // half
    row = jnp.where(core == side, mine[half:half + 1], other[half:half + 1])
    wide = row.shape[1]
    row = pltpu.roll(row, lax.rem(wide - (first - side * half), wide), 1)
    balance_out[...] = row[:, :own]


def work(flops, moved):
    return pl.CostEstimate(flops=flops, bytes_accessed=moved, transcendentals=0)


def call(kernel, outs, *args, placed=True, scratch=(), cost=None):
    shapes = [jax.ShapeDtypeStruct(shape, dtype) for shape, dtype in outs]
    return pl.pallas_call(
        kernel,
        out_shape=shapes,
        in_specs=([SMEM] if placed else []) + [VMEM] * (len(args) - placed),
        out_specs=[VMEM] * len(shapes),
        scratch_shapes=scratch,
        cost_estimate=cost,
    )(*args)


def block_depth(buses, most):
    return max(d for d in range(128, most + 1, 128) if buses % d == 0)


def swap(values):
    return lax.ppermute(values, "core", SWAP)


def on_device(
    ptdf, load, unit_bus, min_up, gen_max, cost_gen, cost_commit, cost_start, init_commit,
    line_limit, gen, commit, startup, line_dual, balance_dual, cap_dual, start_dual, window_dual,
):
    unit_dev, periods = gen.shape
    lines, buses = ptdf.shape
    units = unit_bus.shape[0]
    chips = lax.axis_size("chip")
    half = periods // 2
    unit_chip = 2 * unit_dev
    place = jnp.stack([lax.axis_index("core"), lax.axis_index("chip")])
    every_load = lax.all_gather(load, LINE, axis=0, tiled=True)

    dual_o = swap(line_dual)
    rows_m = call(
        rows_kernel, [((8, lines), F32)], place, line_limit[None], gen_max[None], cost_gen[None],
        balance_dual[None],
    )[0]
    rows_o = swap(rows_m)

    depth = block_depth(buses, 2304)
    cols_m = pl.pallas_call(
        columns_kernel,
        grid=(buses // depth,),
        out_shape=jax.ShapeDtypeStruct((lines, units), BF16),
        in_specs=[
            pl.BlockSpec((1, units), lambda k: (0, 0)),
            pl.BlockSpec((lines, depth), lambda k: (0, k)),
        ],
        out_specs=pl.BlockSpec((lines, units), lambda k: (0, 0)),
        scratch_shapes=[pltpu.VMEM((lines, units), F32)],
        cost_estimate=work(2 * units * lines * buses, ptdf.size * 2),
    )(unit_bus[None], ptdf)
    cols_o = swap(cols_m)

    par = jnp.stack([gen_max, cost_commit, cost_start, init_commit], axis=1)
    square = (unit_dev, periods)
    pack_m, commit1, start1, window1, startup2, grad2, bar_start2, reach2 = call(
        ahead_kernel, [((3 * unit_dev, periods), F32)] + [(square, F32)] * 7, par, min_up[:, None],
        gen, commit, startup, cap_dual, start_dual, window_dual, placed=False,
    )
    pack_o = swap(pack_m)

    blocks = (chips, half, unit_chip)
    parts, dual0, balance0 = call(
        adjoint_kernel, [(blocks, F32), ((half, 2 * lines), F32), ((half, 1), F32)],
        place, cols_m, cols_o, line_dual, dual_o, rows_m, rows_o,
    )
    parts = lax.all_to_all(parts, "chip", 0, 0)
    spread, state_m = call(
        gen1_kernel, [(blocks, BF16), ((2, half, unit_chip), F32)],
        place, parts, pack_m, pack_o, rows_m, rows_o,
    )
    bars = lax.all_to_all(spread, "chip", 0, 0)
    state_o = swap(state_m)

    depth = block_depth(buses, 4608)
    flow_m, send, demand = pl.pallas_call(
        load_kernel,
        grid=(buses // depth,),
        out_shape=[
            jax.ShapeDtypeStruct((half, lines), F32),
            jax.ShapeDtypeStruct((half, lines), F32),
            jax.ShapeDtypeStruct((8, periods), F32),
        ],
        in_specs=[
            SMEM,
            pl.BlockSpec((lines, depth), lambda k: (0, k)),
            pl.BlockSpec((depth, periods), lambda k: (k, 0)),
        ],
        out_specs=[
            pl.BlockSpec((half, lines), lambda k: (0, 0)),
            pl.BlockSpec((half, lines), lambda k: (0, 0)),
            pl.BlockSpec((8, periods), lambda k: (0, 0)),
        ],
        scratch_shapes=[pltpu.VMEM((lines, periods), F32)],
        cost_estimate=work(2 * periods * lines * buses, ptdf.size * 2 + every_load.size * 2),
    )(place, ptdf, every_load)
    flow_o = swap(send)

    held = [pltpu.VMEM((half, units), BF16)]
    parts, dual1, balance1 = call(
        line1_kernel, [(blocks, F32), ((half, 2 * lines), F32), ((half, 1), F32)],
        place, bars, cols_m, cols_o, flow_m, flow_o, dual0, rows_m, rows_o, demand, balance0,
        scratch=held,
    )
    parts = lax.all_to_all(parts, "chip", 0, 0)
    gen1, cap1, bar_commit2, commit2, start2, window2 = call(
        late_kernel, [(square, F32)] * 6,
        place, par, state_m, state_o, commit1, start1, window1, grad2, bar_start2, reach2,
    )
    spread, gen2_m = call(
        gen2_kernel, [(blocks, BF16), ((half, unit_chip), F32)],
        parts, state_m, rows_m, rows_o, placed=False,
    )
    bars = lax.all_to_all(spread, "chip", 0, 0)
    gen2_o = swap(gen2_m)
    gen2, cap2 = call(
        units_kernel, [(square, F32)] * 2, place, par, gen2_m, gen2_o, gen1, cap1, bar_commit2
    )
    dual2, send = call(
        line2_kernel, [((half + 8, lines), F32)] * 2,
        place, bars, cols_m, cols_o, flow_m, flow_o, dual1, rows_m, rows_o, demand, balance1,
        scratch=held,
    )
    dual2, balance2 = call(
        last_kernel, [((lines, periods), F32), ((1, balance_dual.shape[0]), F32)],
        place, dual2, swap(send),
    )
    return (gen2, commit2, startup2, dual2, balance2[0], cap2, start2, window2)


def solution(mesh):
    groups, lines = mesh.devices.shape
    mesh = Mesh(mesh.devices.reshape(groups, lines // 2, 2), ("grp", *LINE))
    wide = P(LINE, "grp")
    unit = P(LINE)
    both = P(("grp", *LINE))
    in_specs = (
        P(LINE, None), wide, P(), unit, unit, unit, unit, unit, unit, unit,
        wide, wide, wide, wide, both, wide, wide, wide,
    )
    out_specs = (wide, wide, wide, wide, both, wide, wide, wide)
    return jax.shard_map(
        on_device, mesh=mesh, in_specs=in_specs, out_specs=out_specs, check_vma=False
    )
```

```python
import functools

import jax
import jax.numpy as jnp
from jax import lax
from jax.experimental import pallas as pl
from jax.experimental.pallas import tpu as pltpu
from jax.sharding import Mesh, PartitionSpec as P

TAU = 0.05
SIGMA = 0.5
SPAN_BITS = 5

F32 = jnp.float32
BF16 = jnp.bfloat16
LINE = ("chip", "core")
SWAP = [(0, 1), (1, 0)]
SLAB_BEFORE = (1, 3, 0, 2)
VMEM = pl.BlockSpec(memory_space=pltpu.VMEM)

LIMIT, GEN_MAX, COST_GEN = 0, 1, 2


def shift_right(values, amount):
    lanes = lax.broadcasted_iota(jnp.int32, values.shape, 1)
    return jnp.where(lanes >= amount, pltpu.roll(values, amount, 1), 0.0)


def shift_left(values, amount):
    periods = values.shape[1]
    lanes = lax.broadcasted_iota(jnp.int32, values.shape, 1)
    return jnp.where(lanes < periods - amount, pltpu.roll(values, periods - amount, 1), 0.0)


def window_sum(values, spans, shift):
    block = values
    total = jnp.zeros_like(values)
    for bit in range(SPAN_BITS):
        chosen = (lax.shift_right_logical(spans, bit) & 1) == 1
        total = jnp.where(chosen, block + shift(total, 1 << bit), total)
        if bit + 1 < SPAN_BITS:
            block = block + shift(block, 1 << bit)
    return total


def diagonal(rows, columns):
    shape = (rows, columns)
    return lax.broadcasted_iota(jnp.int32, shape, 0) == lax.broadcasted_iota(jnp.int32, shape, 1)


def to_column(row):
    size = row.shape[1]
    return jnp.sum(jnp.where(diagonal(size, size), row, 0.0), axis=1, keepdims=True)


def to_row(column):
    size = column.shape[0]
    return jnp.sum(jnp.where(diagonal(size, size), column, 0.0), axis=0, keepdims=True)


def half_of(values, core):
    half = values.shape[0] // 2
    return jnp.where(core == 0, values[:half], values[half:])


def by_core(mine, other, core):
    return jnp.where(
        core == 0,
        jnp.concatenate([mine, other], axis=1),
        jnp.concatenate([other, mine], axis=1),
    )


def rows_kernel(limit, gen_max, cost_gen, out):
    core = lax.axis_index("core")
    wide = out.shape[1]

    def put(row):
        return jnp.concatenate([row, jnp.zeros((1, wide - row.shape[1]), F32)], axis=1)

    units = gen_max.shape[1]
    out[...] = jnp.zeros_like(out)
    out[LIMIT:LIMIT + 1] = limit[...]
    out[GEN_MAX:GEN_MAX + 1] = pltpu.roll(put(gen_max[...]), core * units, 1)
    out[COST_GEN:COST_GEN + 1] = pltpu.roll(put(cost_gen[...]), core * units, 1)


def ahead_kernel(par, spans_ref, gen, commit, startup, cap, start, window,
                 pack, commit1, start1, window1, startup2, grad2, bar_start2, reach2):
    gen_max, cost_commit, cost_start, init = (par[:, i:i + 1] for i in range(4))
    spans = jnp.broadcast_to(spans_ref[...], commit.shape)
    lanes = lax.broadcasted_iota(jnp.int32, commit.shape, 1)
    c0, s0, sd0, wd0 = commit[...], startup[...], start[...], window[...]
    grad_c = cost_commit - gen_max * cap[...] + sd0 - shift_left(sd0, 1) - wd0
    grad_s = cost_start - sd0 + window_sum(wd0, spans, shift_left)
    c1 = jnp.clip(c0 - TAU * grad_c, 0.0, 1.0)
    s1 = jnp.clip(s0 - TAU * grad_s, 0.0, 1.0)
    bc1 = 2.0 * c1 - c0
    bs1 = 2.0 * s1 - s0
    before = jnp.where(lanes == 0, init, pltpu.roll(bc1, 1, 1))
    sd1 = jnp.maximum(0.0, sd0 + SIGMA * (bc1 - before - bs1))
    wd1 = jnp.maximum(0.0, wd0 + SIGMA * (window_sum(bs1, spans, shift_right) - bc1))
    grad_s2 = cost_start - sd1 + window_sum(wd1, spans, shift_left)
    s2 = jnp.clip(s1 - TAU * grad_s2, 0.0, 1.0)
    bs2 = 2.0 * s2 - s1
    units = gen.shape[0]
    pack[0:units] = gen[...]
    pack[units:2 * units] = cap[...]
    pack[2 * units:3 * units] = bc1
    commit1[...] = c1
    start1[...] = sd1
    window1[...] = wd1
    startup2[...] = s2
    grad2[...] = cost_commit + sd1 - shift_left(sd1, 1) - wd1
    bar_start2[...] = bs2
    reach2[...] = window_sum(bs2, spans, shift_right)


def columns_kernel(first, bus, ptdf, *refs):
    *before, cols, acc = refs
    step = pl.program_id(0)
    depth = ptdf.shape[1]
    here = bus[...] - (first + step) * depth
    places = lax.broadcasted_iota(jnp.int32, (depth, bus.shape[1]), 0)
    hot = jnp.where(places == here, 1.0, 0.0).astype(BF16)
    part = jnp.dot(ptdf[...], hot, preferred_element_type=F32)

    @pl.when(step == 0)
    def _():
        acc[...] = before[0][...] + part if before else part

    @pl.when(step > 0)
    def _():
        acc[...] += part

    @pl.when(step == pl.num_programs(0) - 1)
    def _():
        cols[...] = acc[...].astype(cols.dtype)


def put_parts(part, dual, cols_m, cols_o, balance):
    lines = cols_m.shape[0]
    half = dual.astype(BF16)
    total = jnp.dot(half[:, :lines], cols_m[...], preferred_element_type=F32)
    total += jnp.dot(half[:, lines:], cols_o[...], preferred_element_type=F32)
    total += balance
    wide = part.shape[2]
    for i in range(part.shape[0]):
        part[i] = total[:, i * wide:(i + 1) * wide]


def adjoint_kernel(cols_m, cols_o, dual_m, dual_o, balance_m, balance_o, part, dual_t, balance):
    core, chip = lax.axis_index("core"), lax.axis_index("chip")
    periods = dual_m.shape[1]
    dual = jnp.concatenate([half_of(dual_m[...].T, core), half_of(dual_o[...].T, core)], axis=1)
    dual_t[...] = dual
    own = balance_m.shape[1]
    mine, other = balance_m[...], balance_o[...]
    rest = jnp.zeros((1, periods - 2 * own), F32)
    row = jnp.concatenate([by_core(mine, other, core), rest], axis=1)
    row = pltpu.roll(row, 2 * chip * own, 1)
    column = half_of(to_column(row), core)
    balance[...] = column
    put_parts(part, dual, cols_m, cols_o, column)


def gen_step(parts, gen, cap, rows_m, rows_o):
    wide = gen.shape[1]

    def row(i):
        return rows_m[i:i + 1, :wide] + rows_o[i:i + 1, :wide]

    weighted = parts[0]
    for i in range(1, parts.shape[0]):
        weighted = weighted + parts[i]
    gen_max = row(GEN_MAX)
    g1 = jnp.clip(gen - TAU * (row(COST_GEN) + (weighted + cap)), 0.0, gen_max)
    return g1, 2.0 * g1 - gen, gen_max


def gen1_kernel(parts, pack_m, pack_o, rows_m, rows_o, spread, state):
    core = lax.axis_index("core")
    units = pack_m.shape[0] // 3

    def turned(i):
        rows = slice(i * units, (i + 1) * units)
        return by_core(half_of(pack_m[rows].T, core), half_of(pack_o[rows].T, core), core)

    cap = turned(1)
    g1, bar, gen_max = gen_step(parts, turned(0), cap, rows_m, rows_o)
    half = bar.astype(BF16)
    for i in range(spread.shape[0]):
        spread[i] = half
    state[0] = g1
    state[1] = jnp.maximum(0.0, cap + SIGMA * (bar - gen_max * turned(2)))


def gen2_kernel(parts, state, rows_m, rows_o, spread, gen_out):
    g2, bar, _ = gen_step(parts, state[0], state[1], rows_m, rows_o)
    half = bar.astype(BF16)
    for i in range(spread.shape[0]):
        spread[i] = half
    gen_out[...] = g2


def own_units(mine, other, core):
    units = mine.shape[1] // 2
    here, there = mine.T, other.T
    here = jnp.where(core == 0, here[:units], here[units:])
    there = jnp.where(core == 0, there[:units], there[units:])
    return by_core(here, there, core)


def late_kernel(par, state_m, state_o, commit, start, window, grad, bar_start, reach,
                gen1, cap1, bar_commit, commit_out, start_out, window_out):
    core = lax.axis_index("core")
    gen_max, init = par[:, 0:1], par[:, 3:4]
    cap = own_units(state_m[1], state_o[1], core)
    gen1[...] = own_units(state_m[0], state_o[0], core)
    cap1[...] = cap
    lanes = lax.broadcasted_iota(jnp.int32, commit.shape, 1)
    c1 = commit[...]
    c2 = jnp.clip(c1 - TAU * (grad[...] - gen_max * cap), 0.0, 1.0)
    bc2 = 2.0 * c2 - c1
    before = jnp.where(lanes == 0, init, pltpu.roll(bc2, 1, 1))
    commit_out[...] = c2
    bar_commit[...] = bc2
    start_out[...] = jnp.maximum(0.0, start[...] + SIGMA * (bc2 - before - bar_start[...]))
    window_out[...] = jnp.maximum(0.0, window[...] + SIGMA * (reach[...] - bc2))


def units_kernel(par, gen_m, gen_o, gen1, cap1, bar_commit, gen_out, cap_out):
    g2 = own_units(gen_m[...], gen_o[...], lax.axis_index("core"))
    gen_out[...] = g2
    bar = 2.0 * g2 - gen1[...]
    cap_out[...] = jnp.maximum(0.0, cap1[...] + SIGMA * (bar - par[:, 0:1] * bar_commit[...]))


def load_kernel(ptdf, load, keep, send, demand, flow):
    step = pl.program_id(0)
    block = load[...]
    part = jnp.dot(ptdf[...], block, preferred_element_type=F32)
    rows = jnp.sum(block.astype(F32).reshape(-1, 8, block.shape[1]), axis=0)

    @pl.when(step == 0)
    def _():
        flow[...] = part
        demand[...] = rows

    @pl.when(step > 0)
    def _():
        flow[...] += part
        demand[...] += rows

    @pl.when(step == pl.num_programs(0) - 1)
    def _():
        turned = flow[...].T
        core = lax.axis_index("core")
        keep[...] = half_of(turned, core)
        send[...] = half_of(turned, 1 - core)


def slab_kernel(ptdf, *refs):
    pieces, (keep, send, demand, buffers, slab, sems) = refs[:-6], refs[-6:]
    core, chip = lax.axis_index("core"), lax.axis_index("chip")
    side, here = chip % 2, chip // 2
    count, _, depth = buffers.shape
    copies = []
    for i in range(count):
        start = pl.multiple_of(here * depth, depth)
        before = jnp.where(here == 2, SLAB_BEFORE[2], SLAB_BEFORE[3])
        here = jnp.where(here == 0, SLAB_BEFORE[0], jnp.where(here == 1, SLAB_BEFORE[1], before))
        copies.append(
            pltpu.make_async_copy(ptdf.at[:, pl.ds(start, depth)], buffers.at[i], sems.at[i])
        )
        copies[i].start()
    flow, rows = 0.0, 0.0
    for i in range(count):
        near, across, swapped, far = (ref[...] for ref in pieces[4 * i:4 * i + 4])
        bus_dev, periods = near.shape
        for yy in range(2):
            for kk in range(2):
                chosen = jnp.where(
                    side == yy,
                    jnp.where(core == kk, near, swapped),
                    jnp.where(core == kk, across, far),
                )
                at = (2 * yy + kk) * bus_dev
                slab[at:at + bus_dev] = chosen
                rows += jnp.sum(chosen.astype(F32).reshape(-1, 8, periods), axis=0)
        copies[i].wait()
        flow += jnp.dot(buffers[i], slab[...], preferred_element_type=F32)
    turned = flow.T
    keep[...] = half_of(turned, core)
    send[...] = half_of(turned, 1 - core)
    demand[...] = rows


def line_step(bars, cols_m, cols_o, flow_m, flow_o, dual, rows_m, rows_o, held):
    wide = bars.shape[2]
    for i in range(bars.shape[0]):
        held[:, i * wide:(i + 1) * wide] = bars[i]
    bar = held[...]
    turn = (((1,), (1,)), ((), ()))
    mine = lax.dot_general(bar, cols_m[...], turn, preferred_element_type=F32) - flow_m[...]
    other = lax.dot_general(bar, cols_o[...], turn, preferred_element_type=F32) - flow_o[...]
    flows = jnp.concatenate([mine, other], axis=1)
    bound = jnp.concatenate([rows_m[LIMIT:LIMIT + 1], rows_o[LIMIT:LIMIT + 1]], axis=1)
    shifted = dual[...] + SIGMA * flows
    new = shifted - SIGMA * jnp.clip(shifted / SIGMA, -bound, bound)
    totals = jnp.sum(bar.astype(F32), axis=1, keepdims=True)
    return new, totals


def balance_step(totals, demand, balance, units):
    wanted = to_column(jnp.sum(demand[...], axis=0, keepdims=True))
    change = (totals - half_of(wanted, lax.axis_index("core"))) / units
    return balance[...] + change


def line1_kernel(bars, cols_m, cols_o, flow_m, flow_o, dual, rows_m, rows_o, demand,
                 balance, part, dual_out, balance_out, held):
    new, totals = line_step(bars, cols_m, cols_o, flow_m, flow_o, dual, rows_m, rows_o, held)
    dual_out[...] = new
    periods = totals.shape[0]
    own = 2 * periods // part.shape[0]
    rows = lax.broadcasted_iota(jnp.int32, totals.shape, 0) + lax.axis_index("core") * periods
    chip = lax.axis_index("chip")
    held_here = (rows >= chip * own) & (rows < (chip + 1) * own)
    moved = balance_step(totals, demand, balance, cols_m.shape[1])
    moved = jnp.where(held_here, moved, 0.0)
    balance_out[...] = moved
    put_parts(part, new, cols_m, cols_o, moved)


def line2_kernel(bars, cols_m, cols_o, flow_m, flow_o, dual, rows_m, rows_o, demand,
                 balance, keep, send, held):
    new, totals = line_step(bars, cols_m, cols_o, flow_m, flow_o, dual, rows_m, rows_o, held)
    lines, periods = cols_m.shape[0], totals.shape[0]
    moved = to_row(balance_step(totals, demand, balance, cols_m.shape[1]))
    moved = jnp.concatenate([moved, jnp.zeros((1, lines - periods), F32)], axis=1)
    extra = jnp.broadcast_to(moved, (8, lines))
    keep[0:periods] = new[:, :lines]
    keep[periods:] = extra
    send[0:periods] = new[:, lines:]
    send[periods:] = extra


def last_kernel(mine, other, dual_out, balance_out):
    core, chip = lax.axis_index("core"), lax.axis_index("chip")
    half = dual_out.shape[1] // 2
    dual_out[...] = by_core(mine[0:half].T, other[0:half].T, core)
    own = balance_out.shape[1]
    first = (2 * chip + core) * own
    side = first // half
    row = jnp.where(core == side, mine[half:half + 1], other[half:half + 1])
    wide = row.shape[1]
    row = pltpu.roll(row, lax.rem(wide - (first - side * half), wide), 1)
    balance_out[...] = row[:, :own]


def work(flops, moved):
    return pl.CostEstimate(flops=flops, bytes_accessed=moved, transcendentals=0)


def call(kernel, outs, *args, scratch=(), cost=None):
    shapes = [jax.ShapeDtypeStruct(shape, dtype) for shape, dtype in outs]
    return pl.pallas_call(
        kernel,
        out_shape=shapes,
        in_specs=[VMEM] * len(args),
        out_specs=[VMEM] * len(shapes),
        scratch_shapes=scratch,
        cost_estimate=cost,
    )(*args)


def block_depth(buses, most):
    return max(d for d in range(128, most + 1, 128) if buses % d == 0)


def swap(values):
    return lax.ppermute(values, "core", SWAP)


def gathered_product(ptdf, every_load):
    lines, buses = ptdf.shape
    periods = every_load.shape[1]
    half = periods // 2
    depth = block_depth(buses, 4608)
    return pl.pallas_call(
        load_kernel,
        grid=(buses // depth,),
        out_shape=[
            jax.ShapeDtypeStruct((half, lines), F32),
            jax.ShapeDtypeStruct((half, lines), F32),
            jax.ShapeDtypeStruct((8, periods), F32),
        ],
        in_specs=[
            pl.BlockSpec((lines, depth), lambda k: (0, k)),
            pl.BlockSpec((depth, periods), lambda k: (k, 0)),
        ],
        out_specs=[
            pl.BlockSpec((half, lines), lambda k: (0, 0)),
            pl.BlockSpec((half, lines), lambda k: (0, 0)),
            pl.BlockSpec((8, periods), lambda k: (0, 0)),
        ],
        scratch_shapes=[pltpu.VMEM((lines, periods), F32)],
        cost_estimate=work(2 * periods * lines * buses, ptdf.size * 2 + every_load.size * 2),
    )(ptdf, every_load)


def slab_product(ptdf, pieces):
    lines, buses = ptdf.shape
    bus_dev, periods = pieces[0].shape
    count = len(pieces) // 4
    shapes = [((periods // 2, lines), F32)] * 2 + [((8, periods), F32)]
    return pl.pallas_call(
        slab_kernel,
        out_shape=[jax.ShapeDtypeStruct(*shape) for shape in shapes],
        in_specs=[pl.BlockSpec(memory_space=pl.ANY)] + [VMEM] * len(pieces),
        out_specs=[VMEM] * len(shapes),
        scratch_shapes=[
            pltpu.VMEM((count, lines, 4 * bus_dev), BF16),
            pltpu.VMEM((4 * bus_dev, periods), BF16),
            pltpu.SemaphoreType.DMA((count,)),
        ],
        cost_estimate=work(2 * lines * periods * buses, buses * (lines + periods) * 2),
    )(ptdf, *pieces)


def unit_columns(ptdf, unit_bus, first, last, *before):
    lines, buses = ptdf.shape
    units = unit_bus.shape[0]
    depth = block_depth(buses, 2304)
    steps = buses // depth
    kept = BF16 if last == 2 else F32
    start, steps = steps * first // 2, steps * last // 2 - steps * first // 2
    return pl.pallas_call(
        functools.partial(columns_kernel, start),
        grid=(steps,),
        out_shape=jax.ShapeDtypeStruct((lines, units), kept),
        in_specs=[
            pl.BlockSpec((1, units), lambda k: (0, 0)),
            pl.BlockSpec((lines, depth), lambda k: (0, start + k)),
        ] + [pl.BlockSpec((lines, units), lambda k: (0, 0)) for _ in before],
        out_specs=pl.BlockSpec((lines, units), lambda k: (0, 0)),
        scratch_shapes=[pltpu.VMEM((lines, units), F32)],
        cost_estimate=work(2 * units * lines * depth * steps, lines * depth * steps * 2),
    )(unit_bus[None], ptdf, *before)


def on_device(
    ptdf, load, unit_bus, min_up, gen_max, cost_gen, cost_commit, cost_start, init_commit,
    line_limit, gen, commit, startup, line_dual, balance_dual, cap_dual, start_dual, window_dual,
):
    unit_dev, periods = gen.shape
    lines, _ = ptdf.shape
    units = unit_bus.shape[0]
    chips = lax.axis_size("chip")
    half = periods // 2
    unit_chip = 2 * unit_dev
    across = [(i, i ^ 1) for i in range(chips)]
    by_slab = chips == 8 and 4 * load.shape[0] % 128 == 0
    after = lax.optimization_barrier

    def relay(piece):
        pairs = [(2 * SLAB_BEFORE[i // 2] + i % 2, i) for i in range(chips)]
        return lax.ppermute(piece, "chip", pairs)

    def cross(piece):
        return lax.ppermute(piece, "chip", across)

    if by_slab:
        near = [load, relay(load)]
        far = [cross(load)]
    else:
        every_load = lax.all_gather(load, LINE, axis=0, tiled=True)
    dual_o, balance_o = swap(line_dual), swap(balance_dual)

    some = unit_columns(ptdf, unit_bus, 0, 1)
    if by_slab:
        near[1] = after((near[1], some))[0]
        near.append(relay(near[1]))
        far.append(cross(near[1]))
    cols_m = unit_columns(ptdf, unit_bus, 1, 2, some)
    if by_slab:
        near[2] = after((near[2], cols_m))[0]
        near.append(relay(near[2]))
        far.append(cross(near[2]))
    cols_o = swap(cols_m)

    blocks = (chips, half, unit_chip)
    parts, dual0, balance0 = call(
        adjoint_kernel, [(blocks, F32), ((half, 2 * lines), F32), ((half, 1), F32)],
        cols_m, cols_o, line_dual, dual_o, balance_dual[None], balance_o[None],
    )
    commit, startup, gen_max, min_up, parts = after((commit, startup, gen_max, min_up, parts))
    sums = lax.all_to_all(parts, "chip", 0, 0)
    if by_slab:
        near[3] = after((near[3], parts))[0]
        far.append(cross(near[3]))
    rows_m = call(
        rows_kernel, [((8, lines), F32)], line_limit[None], gen_max[None], cost_gen[None]
    )[0]
    rows_o = swap(rows_m)
    par = jnp.stack([gen_max, cost_commit, cost_start, init_commit], axis=1)
    square = (unit_dev, periods)
    pack_m, commit1, start1, window1, startup2, grad2, bar_start2, reach2 = call(
        ahead_kernel, [((3 * unit_dev, periods), F32)] + [(square, F32)] * 7, par,
        min_up[:, None], gen, commit, startup, cap_dual, start_dual, window_dual,
    )
    pack_o = swap(pack_m)
    spread, state_m = call(
        gen1_kernel, [(blocks, BF16), ((2, half, unit_chip), F32)],
        sums, pack_m, pack_o, rows_m, rows_o,
    )

    bars = lax.all_to_all(spread, "chip", 0, 0)
    if by_slab:
        near[2:] = after((*near[2:], spread))[:2]
        far[1:] = after((*far[1:], spread))[:3]
        pieces = [[n, f, swap(n), swap(f)] for n, f in zip(near, far)]
        flow_m, send, demand = slab_product(ptdf, sum(pieces, []))
    else:
        flow_m, send, demand = gathered_product(ptdf, every_load)
    flow_o = swap(send)

    held = [pltpu.VMEM((half, units), BF16)]
    parts, dual1, balance1 = call(
        line1_kernel, [(blocks, F32), ((half, 2 * lines), F32), ((half, 1), F32)],
        bars, cols_m, cols_o, flow_m, flow_o, dual0, rows_m, rows_o, demand, balance0,
        scratch=held,
    )
    sums = lax.all_to_all(parts, "chip", 0, 0)
    state, parts = after((state_m, parts))
    gen1, cap1, bar_commit2, commit2, start2, window2 = call(
        late_kernel, [(square, F32)] * 6,
        par, state, swap(state), commit1, start1, window1, grad2, bar_start2, reach2,
    )
    state_m, bar_commit2 = after((state_m, bar_commit2))
    spread, gen2_m = call(
        gen2_kernel, [(blocks, BF16), ((half, unit_chip), F32)],
        sums, state_m, rows_m, rows_o,
    )
    bars = lax.all_to_all(spread, "chip", 0, 0)
    gen2, cap2 = call(
        units_kernel, [(square, F32)] * 2, par, gen2_m, swap(gen2_m), gen1, cap1, bar_commit2
    )
    dual1, cap2 = after((dual1, cap2))
    dual2, send = call(
        line2_kernel, [((half + 8, lines), F32)] * 2,
        bars, cols_m, cols_o, flow_m, flow_o, dual1, rows_m, rows_o, demand, balance1,
        scratch=held,
    )
    dual2, balance2 = call(
        last_kernel, [((lines, periods), F32), ((1, balance_dual.shape[0]), F32)],
        dual2, swap(send),
    )
    return (gen2, commit2, startup2, dual2, balance2[0], cap2, start2, window2)


def solution(mesh):
    groups, lines = mesh.devices.shape
    mesh = Mesh(mesh.devices.reshape(groups, lines // 2, 2), ("grp", *LINE))
    wide = P(LINE, "grp")
    unit = P(LINE)
    both = P(("grp", *LINE))
    in_specs = (
        P(LINE, None), wide, P(), unit, unit, unit, unit, unit, unit, unit,
        wide, wide, wide, wide, both, wide, wide, wide,
    )
    out_specs = (wide, wide, wide, wide, both, wide, wide, wide)

    return jax.shard_map(
        on_device, mesh=mesh, in_specs=in_specs, out_specs=out_specs, check_vma=False
    )
```

```python
import jax
import jax.numpy as jnp
from jax import lax
from jax.experimental import pallas as pl
from jax.experimental.pallas import tpu as pltpu
from jax.sharding import Mesh, PartitionSpec as P

TAU = 0.05
SIGMA = 0.5
SPAN_BITS = 5

F32 = jnp.float32
BF16 = jnp.bfloat16
LINE = ("chip", "core")
SWAP = [(0, 1), (1, 0)]
VMEM = pl.BlockSpec(memory_space=pltpu.VMEM)
HBM = pl.BlockSpec(memory_space=pltpu.HBM)


def shift_right(values, amount):
    lanes = lax.broadcasted_iota(jnp.int32, values.shape, 1)
    return jnp.where(lanes >= amount, pltpu.roll(values, amount, 1), 0.0)


def shift_left(values, amount):
    periods = values.shape[1]
    lanes = lax.broadcasted_iota(jnp.int32, values.shape, 1)
    return jnp.where(lanes < periods - amount, pltpu.roll(values, periods - amount, 1), 0.0)


def window_sum(values, spans, shift):
    block = values
    total = jnp.zeros_like(values)
    for bit in range(SPAN_BITS):
        chosen = (lax.shift_right_logical(spans, bit) & 1) == 1
        total = jnp.where(chosen, block + shift(total, 1 << bit), total)
        if bit + 1 < SPAN_BITS:
            block = block + shift(block, 1 << bit)
    return total


def diagonal(rows, columns):
    shape = (rows, columns)
    return lax.broadcasted_iota(jnp.int32, shape, 0) == lax.broadcasted_iota(jnp.int32, shape, 1)


def to_column(row):
    size = row.shape[1]
    return jnp.sum(jnp.where(diagonal(size, size), row, 0.0), axis=1, keepdims=True)


def to_row(column):
    size = column.shape[0]
    return jnp.sum(jnp.where(diagonal(size, size), column, 0.0), axis=0, keepdims=True)


def half_of(values, core):
    half = values.shape[0] // 2
    return jnp.where(core == 0, values[:half], values[half:])


def by_core(mine, other, core):
    return jnp.where(
        core == 0,
        jnp.concatenate([mine, other], axis=1),
        jnp.concatenate([other, mine], axis=1),
    )


def packed_row(mine, other, index):
    at = mine.shape[0] - 8 + index
    return mine[at:at + 1] + other[at:at + 1]


def packed_limits(mine, other, lines):
    rows = []
    for pack in (mine, other):
        for i in range(lines // pack.shape[1]):
            at = pack.shape[0] - 6 + i
            rows.append(pack[at:at + 1])
    return jnp.concatenate(rows, axis=1)


def ahead_kernel(par, gen_row, cost_row, limit, gen, commit, startup, cap, start, window,
                 pack, startup2, hold):
    gen_max, cost_commit, cost_start, init = (par[:, i:i + 1] for i in range(4))
    spans = jnp.broadcast_to(par[:, 4:5].astype(jnp.int32), commit.shape)
    lanes = lax.broadcasted_iota(jnp.int32, commit.shape, 1)
    c0, s0, sd0, wd0 = commit[...], startup[...], start[...], window[...]
    grad_c = cost_commit - gen_max * cap[...] + sd0 - shift_left(sd0, 1) - wd0
    grad_s = cost_start - sd0 + window_sum(wd0, spans, shift_left)
    c1 = jnp.clip(c0 - TAU * grad_c, 0.0, 1.0)
    s1 = jnp.clip(s0 - TAU * grad_s, 0.0, 1.0)
    bc1 = 2.0 * c1 - c0
    bs1 = 2.0 * s1 - s0
    before = jnp.where(lanes == 0, init, pltpu.roll(bc1, 1, 1))
    sd1 = jnp.maximum(0.0, sd0 + SIGMA * (bc1 - before - bs1))
    wd1 = jnp.maximum(0.0, wd0 + SIGMA * (window_sum(bs1, spans, shift_right) - bc1))
    grad_s2 = cost_start - sd1 + window_sum(wd1, spans, shift_left)
    s2 = jnp.clip(s1 - TAU * grad_s2, 0.0, 1.0)
    bs2 = 2.0 * s2 - s1
    units = gen.shape[0]
    pack[0:units] = gen[...]
    pack[units:2 * units] = cap[...]
    pack[2 * units:3 * units] = bc1
    core, wide = lax.axis_index("core"), pack.shape[1]
    blank = jnp.zeros((1, wide - units), F32)
    table = [pltpu.roll(jnp.concatenate([row[...], blank], axis=1), core * units, 1)
             for row in (gen_row, cost_row)]
    table += [limit[:, i:i + wide] for i in range(0, limit.shape[1], wide)]
    table += [jnp.zeros((1, wide), F32)] * (8 - len(table))
    pack[3 * units:] = jnp.concatenate(table, axis=0)
    startup2[...] = s2
    hold[0] = c1
    hold[1] = cost_commit + sd1 - shift_left(sd1, 1) - wd1
    hold[2] = sd1 - SIGMA * bs2
    hold[3] = wd1 + SIGMA * window_sum(bs2, spans, shift_right)


def columns_kernel(bus, ptdf, cols, acc):
    step = pl.program_id(0)
    depth = ptdf.shape[1]
    here = bus[...] - step * depth
    places = lax.broadcasted_iota(jnp.int32, (depth, bus.shape[1]), 0)
    hot = jnp.where(places == here, 1.0, 0.0).astype(BF16)
    part = jnp.dot(ptdf[...], hot, preferred_element_type=F32)

    @pl.when(step == 0)
    def _():
        acc[...] = part

    @pl.when(step > 0)
    def _():
        acc[...] += part

    @pl.when(step == pl.num_programs(0) - 1)
    def _():
        cols[...] = acc[...].astype(BF16)


def put_parts(part, dual, cols_m, cols_o, balance):
    lines = cols_m.shape[0]
    half = dual.astype(BF16)
    total = jnp.dot(half[:, :lines], cols_m[...], preferred_element_type=F32)
    total += jnp.dot(half[:, lines:], cols_o[...], preferred_element_type=F32)
    total += balance
    wide = part.shape[2]
    for i in range(part.shape[0]):
        part[i] = total[:, i * wide:(i + 1) * wide]


def adjoint_kernel(cols_m, cols_o, dual_m, dual_o, balance_m, balance_o, part, dual_t, balance):
    core, chip = lax.axis_index("core"), lax.axis_index("chip")
    periods = dual_m.shape[1]
    dual = jnp.concatenate([half_of(dual_m[...].T, core), half_of(dual_o[...].T, core)], axis=1)
    dual_t[...] = dual
    own = balance_m.shape[1]
    mine, other = balance_m[...], balance_o[...]
    rest = jnp.zeros((1, periods - 2 * own), F32)
    row = jnp.concatenate([by_core(mine, other, core), rest], axis=1)
    row = pltpu.roll(row, 2 * chip * own, 1)
    column = half_of(to_column(row), core)
    balance[...] = column
    put_parts(part, dual, cols_m, cols_o, column)


def gen_step(parts, gen, cap, pack_m, pack_o):
    weighted = parts[0]
    for i in range(1, parts.shape[0]):
        weighted = weighted + parts[i]
    gen_max = packed_row(pack_m, pack_o, 0)
    cost_gen = packed_row(pack_m, pack_o, 1)
    g1 = jnp.clip(gen - TAU * (cost_gen + (weighted + cap)), 0.0, gen_max)
    return g1, 2.0 * g1 - gen, gen_max


def gen1_kernel(parts, pack_m, pack_o, spread, state):
    core = lax.axis_index("core")
    units = (pack_m.shape[0] - 8) // 3

    def turned(i):
        rows = slice(i * units, (i + 1) * units)
        return by_core(half_of(pack_m[rows].T, core), half_of(pack_o[rows].T, core), core)

    cap = turned(1)
    g1, bar, gen_max = gen_step(parts, turned(0), cap, pack_m, pack_o)
    half = bar.astype(BF16)
    for i in range(spread.shape[0]):
        spread[i] = half
    state[0] = g1
    state[1] = jnp.maximum(0.0, cap + SIGMA * (bar - gen_max * turned(2)))


def gen2_kernel(parts, state, pack_m, pack_o, spread, gen_out):
    g2, bar, _ = gen_step(parts, state[0], state[1], pack_m, pack_o)
    half = bar.astype(BF16)
    for i in range(spread.shape[0]):
        spread[i] = half
    gen_out[...] = g2


def own_units(mine, other, core):
    units = mine.shape[1] // 2
    here, there = mine.T, other.T
    here = jnp.where(core == 0, here[:units], here[units:])
    there = jnp.where(core == 0, there[:units], there[units:])
    return by_core(here, there, core)


def late_kernel(par, state_m, state_o, keep, other, hold,
                gen1, cap1, bar_commit, dual, balance, commit_out, start_out, window_out):
    core = lax.axis_index("core")
    gen_max, init = par[:, 0:1], par[:, 3:4]
    cap = own_units(state_m[1], state_o[1], core)
    gen1[...] = own_units(state_m[0], state_o[0], core)
    half = dual.shape[1] // 2
    dual[...] = by_core(keep[0:half].T, other[0:half].T, core)
    own = balance.shape[1]
    first = (2 * lax.axis_index("chip") + core) * own
    side = first // half
    row = jnp.where(core == side, keep[half:half + 1], other[half:half + 1])
    wide = row.shape[1]
    row = pltpu.roll(row, lax.rem(wide - (first - side * half), wide), 1)
    balance[...] = row[:, :own]
    cap1[...] = cap
    c1, grad, start, window = (hold[i] for i in range(4))
    lanes = lax.broadcasted_iota(jnp.int32, c1.shape, 1)
    c2 = jnp.clip(c1 - TAU * (grad - gen_max * cap), 0.0, 1.0)
    bc2 = 2.0 * c2 - c1
    before = jnp.where(lanes == 0, init, pltpu.roll(bc2, 1, 1))
    commit_out[...] = c2
    bar_commit[...] = bc2
    start_out[...] = jnp.maximum(0.0, start + SIGMA * (bc2 - before))
    window_out[...] = jnp.maximum(0.0, window - SIGMA * bc2)


def units_kernel(par, gen_m, gen_o, gen1, cap1, bar_commit, gen_out, cap_out):
    g2 = own_units(gen_m[...], gen_o[...], lax.axis_index("core"))
    gen_out[...] = g2
    bar = 2.0 * g2 - gen1[...]
    cap_out[...] = jnp.maximum(0.0, cap1[...] + SIGMA * (bar - par[:, 0:1] * bar_commit[...]))


def load_kernel(ptdf, load, keep, send, demand, flow):
    step = pl.program_id(0)
    block = load[...]
    part = jnp.dot(ptdf[...], block, preferred_element_type=F32)
    rows = jnp.sum(block.astype(F32).reshape(-1, 8, block.shape[1]), axis=0)

    @pl.when(step == 0)
    def _():
        flow[...] = part
        demand[...] = rows

    @pl.when(step > 0)
    def _():
        flow[...] += part
        demand[...] += rows

    @pl.when(step == pl.num_programs(0) - 1)
    def _():
        turned = flow[...].T
        core = lax.axis_index("core")
        keep[...] = half_of(turned, core)
        send[...] = half_of(turned, 1 - core)


def slab_kernel(ptdf, *refs):
    pieces, (keep, send, demand, total, slab, buffers, sems) = refs[:-7], refs[-7:]
    core, chip = lax.axis_index("core"), lax.axis_index("chip")
    side, here = chip % 2, chip // 2
    depth = slab.shape[0]
    copies = []
    for i in range(len(pieces) // 4):
        start = pl.multiple_of(jnp.bitwise_xor(here, i) * depth, depth)
        copies.append(
            pltpu.make_async_copy(ptdf.at[:, pl.ds(start, depth)], buffers.at[i], sems.at[i])
        )
        copies[i].start()
    flow, rows = 0.0, 0.0
    for i in range(len(pieces) // 4):
        near, across, swapped, far = (ref[...] for ref in pieces[4 * i:4 * i + 4])
        bus_dev, periods = near.shape
        for yy in range(2):
            for kk in range(2):
                chosen = jnp.where(
                    side == yy,
                    jnp.where(core == kk, near, swapped),
                    jnp.where(core == kk, across, far),
                )
                at = (2 * yy + kk) * bus_dev
                slab[at:at + bus_dev] = chosen
                rows += jnp.sum(chosen.astype(F32).reshape(-1, 8, periods), axis=0)
        copies[i].wait()
        flow += jnp.dot(buffers[i], slab[...], preferred_element_type=F32)
    total[...] = flow
    turned = flow.T
    keep[...] = half_of(turned, core)
    send[...] = half_of(turned, 1 - core)
    demand[...] = rows


def line_step(flows, dual, bound):
    shifted = dual + SIGMA * flows
    return shifted - SIGMA * jnp.clip(shifted / SIGMA, -bound, bound)


def balance_change(bar, demand, units):
    totals = jnp.sum(bar.astype(F32), axis=1, keepdims=True)
    return (totals - demand) / units


TURN = (((1,), (1,)), ((), ()))


def line1_kernel(bars, cols_m, cols_o, flow_m, flow_o, dual, pack_m, pack_o, demand,
                 balance, part, keep, send, held):
    core, chip = lax.axis_index("core"), lax.axis_index("chip")
    lines, units = cols_m.shape
    wide = bars.shape[2]
    for i in range(bars.shape[0]):
        held[:, i * wide:(i + 1) * wide] = bars[i]
    bar = held[...]
    mine = lax.dot_general(bar, cols_m[...], TURN, preferred_element_type=F32) - flow_m[...]
    other = lax.dot_general(bar, cols_o[...], TURN, preferred_element_type=F32) - flow_o[...]
    flows = jnp.concatenate([mine, other], axis=1)
    new = line_step(flows, dual[...], packed_limits(pack_m, pack_o, lines))
    wanted = half_of(to_column(jnp.sum(demand[...], axis=0, keepdims=True)), core)
    moved = balance[...] + balance_change(bar, wanted, units)
    periods = moved.shape[0]
    own = 2 * periods // part.shape[0]
    rows = lax.broadcasted_iota(jnp.int32, moved.shape, 0) + core * periods
    moved = jnp.where((rows >= chip * own) & (rows < (chip + 1) * own), moved, 0.0)
    put_parts(part, new, cols_m, cols_o, moved)
    row = jnp.concatenate([to_row(moved), jnp.zeros((1, lines - periods), F32)], axis=1)
    extra = jnp.broadcast_to(row, (8, lines))
    keep[0:periods] = new[:, :lines]
    keep[periods:] = extra
    send[0:periods] = new[:, lines:]
    send[periods:] = extra


def line2_kernel(bars_m, bars_o, cols, flow, dual, limit, demand, balance, dual_out, balance_out,
                 held):
    core, chip = lax.axis_index("core"), lax.axis_index("chip")
    half, wide = bars_m.shape[1:]
    for i in range(bars_m.shape[0]):
        here, there = bars_m[i], bars_o[i]
        held[0:half, i * wide:(i + 1) * wide] = jnp.where(core == 0, here, there)
        held[half:, i * wide:(i + 1) * wide] = jnp.where(core == 0, there, here)
    bar = held[...]
    flows = lax.dot_general(cols[...], bar, TURN, preferred_element_type=F32) - flow[...]
    dual_out[...] = line_step(flows, dual[...], limit[...])
    wanted = to_column(jnp.sum(demand[...], axis=0, keepdims=True))
    change = to_row(balance_change(bar, wanted, cols.shape[1]))
    own = balance_out.shape[1]
    first = (2 * chip + core) * own
    wide = change.shape[1]
    change = pltpu.roll(change, lax.rem(wide - first, wide), 1)
    balance_out[...] = balance[...] + change[:, :own]


def work(flops, moved):
    return pl.CostEstimate(flops=flops, bytes_accessed=moved, transcendentals=0)


def room(mib):
    return pltpu.CompilerParams(vmem_limit_bytes=mib << 20)


def call(kernel, outs, *args, scratch=(), cost=None):
    shapes = [jax.ShapeDtypeStruct(shape, dtype) for shape, dtype in outs]
    return pl.pallas_call(
        kernel,
        out_shape=shapes,
        in_specs=[VMEM] * len(args),
        out_specs=[VMEM] * len(shapes),
        scratch_shapes=scratch,
        cost_estimate=cost,
        compiler_params=room(8),
    )(*args)


def block_depth(buses, most):
    return max(d for d in range(128, most + 1, 128) if buses % d == 0)


def swap(values):
    return lax.ppermute(values, "core", SWAP)


def gathered_product(ptdf, every_load):
    lines, buses = ptdf.shape
    periods = every_load.shape[1]
    half = periods // 2
    depth = block_depth(buses, 4608)
    return pl.pallas_call(
        load_kernel,
        grid=(buses // depth,),
        out_shape=[
            jax.ShapeDtypeStruct((half, lines), F32),
            jax.ShapeDtypeStruct((half, lines), F32),
            jax.ShapeDtypeStruct((8, periods), F32),
            jax.ShapeDtypeStruct((lines, periods), F32),
        ],
        in_specs=[
            pl.BlockSpec((lines, depth), lambda k: (0, k)),
            pl.BlockSpec((depth, periods), lambda k: (k, 0)),
        ],
        out_specs=[
            pl.BlockSpec((half, lines), lambda k: (0, 0)),
            pl.BlockSpec((half, lines), lambda k: (0, 0)),
            pl.BlockSpec((8, periods), lambda k: (0, 0)),
            pl.BlockSpec((lines, periods), lambda k: (0, 0)),
        ],
        cost_estimate=work(2 * periods * lines * buses, ptdf.size * 2 + every_load.size * 2),
    )(ptdf, every_load)


def slab_product(ptdf, pieces):
    lines, buses = ptdf.shape
    bus_dev, periods = pieces[0].shape
    shapes = [((periods // 2, lines), F32)] * 2 + [((8, periods), F32), ((lines, periods), F32)]
    return pl.pallas_call(
        slab_kernel,
        out_shape=[jax.ShapeDtypeStruct(*shape) for shape in shapes],
        in_specs=[HBM] + [VMEM] * len(pieces),
        out_specs=[VMEM] * len(shapes),
        scratch_shapes=[
            pltpu.VMEM((4 * bus_dev, periods), BF16),
            pltpu.VMEM((len(pieces) // 4, lines, 4 * bus_dev), BF16),
            pltpu.SemaphoreType.DMA((len(pieces) // 4,)),
        ],
        cost_estimate=work(2 * lines * periods * buses, buses * (lines + periods) * 2),
        compiler_params=room(16),
    )(ptdf, *pieces)


def unit_columns(ptdf, unit_bus):
    lines, buses = ptdf.shape
    units = unit_bus.shape[0]
    depth = block_depth(buses, 2304)
    return pl.pallas_call(
        columns_kernel,
        grid=(buses // depth,),
        out_shape=jax.ShapeDtypeStruct((lines, units), BF16),
        in_specs=[
            pl.BlockSpec((1, units), lambda k: (0, 0)),
            pl.BlockSpec((lines, depth), lambda k: (0, k)),
        ],
        out_specs=pl.BlockSpec((lines, units), lambda k: (0, 0)),
        scratch_shapes=[pltpu.VMEM((lines, units), F32)],
        cost_estimate=work(2 * units * lines * buses, ptdf.size * 2),
        compiler_params=room(24),
    )(unit_bus[None], ptdf)


def on_device(
    ptdf, load, unit_bus, min_up, gen_max, cost_gen, cost_commit, cost_start, init_commit,
    line_limit, gen, commit, startup, line_dual, balance_dual, cap_dual, start_dual, window_dual,
):
    unit_dev, periods = gen.shape
    lines, _ = ptdf.shape
    units = unit_bus.shape[0]
    chips = lax.axis_size("chip")
    half = periods // 2
    unit_chip = 2 * unit_dev
    across = [(i, i ^ 1) for i in range(chips)]
    by_slab = chips == 8 and 4 * load.shape[0] % 128 == 0
    after = lax.optimization_barrier

    def along(turn):
        pairs = [(i, i ^ 2 * turn) for i in range(chips)]
        return lax.ppermute(load, "chip", pairs)

    def cross(piece):
        return lax.ppermute(piece, "chip", across)

    if by_slab:
        near = [load, along(1), along(2), along(3)]
        far = [cross(load)]
    else:
        every_load = lax.all_gather(load, LINE, axis=0, tiled=True)
    dual_o, balance_o = swap(line_dual), swap(balance_dual)
    ptdf = pltpu.with_memory_space_constraint(ptdf, pltpu.HBM)

    cols_m = unit_columns(ptdf, unit_bus)
    if by_slab:
        near[1] = after((near[1], cols_m))[0]
        far.append(cross(near[1]))
    cols_o = swap(cols_m)

    blocks = (chips, half, unit_chip)
    parts, dual0, balance0 = call(
        adjoint_kernel, [(blocks, F32), ((half, 2 * lines), F32), ((half, 1), F32)],
        cols_m, cols_o, line_dual, dual_o, balance_dual[None], balance_o[None],
    )
    commit, startup, gen_max, min_up, parts = after((commit, startup, gen_max, min_up, parts))
    sums = lax.all_to_all(parts, "chip", 0, 0)
    if by_slab:
        near[2:] = after((*near[2:], parts))[:2]
        far.append(cross(near[2]))
        far.append(cross(near[3]))
    par = jnp.stack(
        [gen_max, cost_commit, cost_start, init_commit, min_up.astype(F32)], axis=1
    )
    square = (unit_dev, periods)
    pack_m, startup2, hold = call(
        ahead_kernel,
        [((3 * unit_dev + 8, periods), F32), (square, F32), ((4, *square), F32)], par,
        gen_max[None], cost_gen[None], line_limit[None], gen, commit, startup, cap_dual, start_dual, window_dual,
    )
    pack_o = swap(pack_m)
    spread, state_m = call(
        gen1_kernel, [(blocks, BF16), ((2, half, unit_chip), F32)],
        sums, pack_m, pack_o,
    )

    bars = lax.all_to_all(spread, "chip", 0, 0)
    if by_slab:
        far[2:] = after((*far[2:], spread))[:2]
        near_o = [swap(piece) for piece in near]
        far_o = [swap(piece) for piece in far[:2]]
        far_o += [swap(piece) for piece in far[2:]]
        pieces = [list(four) for four in zip(near, far, near_o, far_o)]
        flow_m, send, demand, flow = slab_product(ptdf, sum(pieces, []))
    else:
        flow_m, send, demand, flow = gathered_product(ptdf, every_load)
    flow_o = swap(send)

    parts, keep, send = call(
        line1_kernel, [(blocks, F32)] + [((half + 8, lines), F32)] * 2,
        bars, cols_m, cols_o, flow_m, flow_o, dual0, pack_m, pack_o, demand, balance0,
        scratch=[pltpu.VMEM((half, units), BF16)],
    )
    sums = lax.all_to_all(parts, "chip", 0, 0)
    state, par, line_limit, parts = after((state_m, par, line_limit, parts))
    limit = line_limit[:, None]
    small = ((1, balance_dual.shape[0]), F32)
    state_o, dual_o = swap(state), swap(send)
    gen1, cap1, bar_commit2, dual1, balance1, commit2, start2, window2 = call(
        late_kernel,
        [(square, F32)] * 3 + [((lines, periods), F32), small] + [(square, F32)] * 3,
        par, state, state_o, keep, dual_o, hold,
    )
    state_m, bar_commit2, limit = after((state_m, bar_commit2, limit))
    spread, gen2_m = call(
        gen2_kernel, [(blocks, BF16), ((half, unit_chip), F32)], sums, state_m, pack_m, pack_o,
    )
    bars = lax.all_to_all(spread, "chip", 0, 0)
    gen2_o = swap(gen2_m)
    gen2, cap2 = call(
        units_kernel, [(square, F32)] * 2, par, gen2_m, gen2_o, gen1, cap1, bar_commit2
    )
    dual1, cap2 = after((dual1, cap2))
    dual2, balance2 = call(
        line2_kernel, [((lines, periods), F32), small],
        bars, swap(bars), cols_m, flow, dual1, limit, demand, balance1,
        scratch=[pltpu.VMEM((periods, units), BF16)],
    )
    return (gen2, commit2, startup2, dual2, balance2[0], cap2, start2, window2)


def solution(mesh):
    groups, lines = mesh.devices.shape
    mesh = Mesh(mesh.devices.reshape(groups, lines // 2, 2), ("grp", *LINE))
    wide = P(LINE, "grp")
    unit = P(LINE)
    both = P(("grp", *LINE))
    in_specs = (
        P(LINE, None), wide, P(), unit, unit, unit, unit, unit, unit, unit,
        wide, wide, wide, wide, both, wide, wide, wide,
    )
    out_specs = (wide, wide, wide, wide, both, wide, wide, wide)

    return jax.shard_map(
        on_device, mesh=mesh, in_specs=in_specs, out_specs=out_specs, check_vma=False
    )
```

```python
import jax
import jax.numpy as jnp
from jax import lax
from jax.experimental import pallas as pl
from jax.experimental.pallas import tpu as pltpu
from jax.sharding import Mesh, PartitionSpec as P

TAU = 0.05
SIGMA = 0.5
SPAN_BITS = 5

F32 = jnp.float32
BF16 = jnp.bfloat16
LINE = ("chip", "core")
SWAP = [(0, 1), (1, 0)]
VMEM = pl.BlockSpec(memory_space=pltpu.VMEM)
HBM = pl.BlockSpec(memory_space=pltpu.HBM)


def shift_right(values, amount):
    lanes = lax.broadcasted_iota(jnp.int32, values.shape, 1)
    return jnp.where(lanes >= amount, pltpu.roll(values, amount, 1), 0.0)


def shift_left(values, amount):
    periods = values.shape[1]
    lanes = lax.broadcasted_iota(jnp.int32, values.shape, 1)
    return jnp.where(lanes < periods - amount, pltpu.roll(values, periods - amount, 1), 0.0)


def window_sum(values, spans, shift):
    block = values
    total = jnp.zeros_like(values)
    for bit in range(SPAN_BITS):
        chosen = (lax.shift_right_logical(spans, bit) & 1) == 1
        total = jnp.where(chosen, block + shift(total, 1 << bit), total)
        if bit + 1 < SPAN_BITS:
            block = block + shift(block, 1 << bit)
    return total


def diagonal(rows, columns):
    shape = (rows, columns)
    return lax.broadcasted_iota(jnp.int32, shape, 0) == lax.broadcasted_iota(jnp.int32, shape, 1)


def to_column(row):
    size = row.shape[1]
    return jnp.sum(jnp.where(diagonal(size, size), row, 0.0), axis=1, keepdims=True)


def to_row(column):
    size = column.shape[0]
    return jnp.sum(jnp.where(diagonal(size, size), column, 0.0), axis=0, keepdims=True)


def half_of(values, core):
    half = values.shape[0] // 2
    return jnp.where(core == 0, values[:half], values[half:])


def by_core(mine, other, core):
    return jnp.where(
        core == 0,
        jnp.concatenate([mine, other], axis=1),
        jnp.concatenate([other, mine], axis=1),
    )


def packed_row(mine, other, index):
    at = mine.shape[0] - 8 + index
    return mine[at:at + 1] + other[at:at + 1]


def packed_limits(mine, other, lines):
    rows = []
    for pack in (mine, other):
        for i in range(lines // pack.shape[1]):
            at = pack.shape[0] - 6 + i
            rows.append(pack[at:at + 1])
    return jnp.concatenate(rows, axis=1)


def ahead_kernel(par, gen_row, cost_row, limit, balance, gen, commit, startup, cap, start, window,
                 pack, startup2, hold):
    gen_max, cost_commit, cost_start, init = (par[:, i:i + 1] for i in range(4))
    spans = jnp.broadcast_to(par[:, 4:5].astype(jnp.int32), commit.shape)
    lanes = lax.broadcasted_iota(jnp.int32, commit.shape, 1)
    c0, s0, sd0, wd0 = commit[...], startup[...], start[...], window[...]
    grad_c = cost_commit - gen_max * cap[...] + sd0 - shift_left(sd0, 1) - wd0
    grad_s = cost_start - sd0 + window_sum(wd0, spans, shift_left)
    c1 = jnp.clip(c0 - TAU * grad_c, 0.0, 1.0)
    s1 = jnp.clip(s0 - TAU * grad_s, 0.0, 1.0)
    bc1 = 2.0 * c1 - c0
    bs1 = 2.0 * s1 - s0
    before = jnp.where(lanes == 0, init, pltpu.roll(bc1, 1, 1))
    sd1 = jnp.maximum(0.0, sd0 + SIGMA * (bc1 - before - bs1))
    wd1 = jnp.maximum(0.0, wd0 + SIGMA * (window_sum(bs1, spans, shift_right) - bc1))
    grad_s2 = cost_start - sd1 + window_sum(wd1, spans, shift_left)
    s2 = jnp.clip(s1 - TAU * grad_s2, 0.0, 1.0)
    bs2 = 2.0 * s2 - s1
    units = gen.shape[0]
    pack[0:units] = gen[...]
    pack[units:2 * units] = cap[...]
    pack[2 * units:3 * units] = bc1
    core, wide = lax.axis_index("core"), pack.shape[1]
    blank = jnp.zeros((1, wide - units), F32)
    table = [pltpu.roll(jnp.concatenate([row[...], blank], axis=1), core * units, 1)
             for row in (gen_row, cost_row)]
    table += [limit[:, i:i + wide] for i in range(0, limit.shape[1], wide)]
    own = balance.shape[1]
    row = jnp.concatenate([balance[...], jnp.zeros((1, wide - own), F32)], axis=1)
    table.append(pltpu.roll(row, (2 * lax.axis_index("chip") + core) * own, 1))
    table += [jnp.zeros((1, wide), F32)] * (8 - len(table))
    pack[3 * units:] = jnp.concatenate(table, axis=0)
    startup2[...] = s2
    hold[0] = c1
    hold[1] = cost_commit + sd1 - shift_left(sd1, 1) - wd1
    hold[2] = sd1 - SIGMA * bs2
    hold[3] = wd1 + SIGMA * window_sum(bs2, spans, shift_right)


def columns_kernel(bus, ptdf, cols, acc):
    step = pl.program_id(0)
    depth = ptdf.shape[1]
    here = bus[...] - step * depth
    places = lax.broadcasted_iota(jnp.int32, (depth, bus.shape[1]), 0)
    hot = jnp.where(places == here, 1.0, 0.0).astype(BF16)
    part = jnp.dot(ptdf[...], hot, preferred_element_type=F32)

    @pl.when(step == 0)
    def _():
        acc[...] = part

    @pl.when(step > 0)
    def _():
        acc[...] += part

    @pl.when(step == pl.num_programs(0) - 1)
    def _():
        cols[...] = acc[...].astype(BF16)


def put_parts(part, dual, cols_m, cols_o, balance):
    lines = cols_m.shape[0]
    half = dual.astype(BF16)
    total = jnp.dot(half[:, :lines], cols_m[...], preferred_element_type=F32)
    total += jnp.dot(half[:, lines:], cols_o[...], preferred_element_type=F32)
    total += balance
    wide = part.shape[2]
    for i in range(part.shape[0]):
        part[i] = total[:, i * wide:(i + 1) * wide]


def balance_column(mine, other, periods):
    core, chip = lax.axis_index("core"), lax.axis_index("chip")
    own = mine.shape[1]
    rest = jnp.zeros((1, periods - 2 * own), F32)
    row = jnp.concatenate([by_core(mine[...], other[...], core), rest], axis=1)
    return half_of(to_column(pltpu.roll(row, 2 * chip * own, 1)), core)


def adjoint_kernel(cols_m, cols_o, dual_m, dual_o, balance_m, balance_o, part, dual_t):
    core = lax.axis_index("core")
    dual = jnp.concatenate([half_of(dual_m[...].T, core), half_of(dual_o[...].T, core)], axis=1)
    dual_t[...] = dual
    column = balance_column(balance_m, balance_o, dual_m.shape[1])
    put_parts(part, dual, cols_m, cols_o, column)


def gen_step(parts, gen, cap, pack_m, pack_o):
    weighted = parts[0]
    for i in range(1, parts.shape[0]):
        weighted = weighted + parts[i]
    gen_max = packed_row(pack_m, pack_o, 0)
    cost_gen = packed_row(pack_m, pack_o, 1)
    g1 = jnp.clip(gen - TAU * (cost_gen + (weighted + cap)), 0.0, gen_max)
    return g1, 2.0 * g1 - gen, gen_max


def gen1_kernel(parts, pack_m, pack_o, spread, state):
    core = lax.axis_index("core")
    units = (pack_m.shape[0] - 8) // 3

    def turned(i):
        rows = slice(i * units, (i + 1) * units)
        return by_core(half_of(pack_m[rows].T, core), half_of(pack_o[rows].T, core), core)

    cap = turned(1)
    g1, bar, gen_max = gen_step(parts, turned(0), cap, pack_m, pack_o)
    half = bar.astype(BF16)
    for i in range(spread.shape[0]):
        spread[i] = half
    state[0] = g1
    state[1] = jnp.maximum(0.0, cap + SIGMA * (bar - gen_max * turned(2)))


def gen2_kernel(parts, state, pack_m, pack_o, spread, gen_out):
    g2, bar, _ = gen_step(parts, state[0], state[1], pack_m, pack_o)
    half = bar.astype(BF16)
    for i in range(spread.shape[0]):
        spread[i] = half
    gen_out[...] = g2


def own_units(mine, other, core):
    units = mine.shape[1] // 2
    here, there = mine.T, other.T
    here = jnp.where(core == 0, here[:units], here[units:])
    there = jnp.where(core == 0, there[:units], there[units:])
    return by_core(here, there, core)


def late_kernel(par, state_m, state_o, keep, other, hold, flow_m, flow_s,
                flow, gen1, cap1, bar_commit, dual, balance, commit_out, start_out, window_out):
    core = lax.axis_index("core")
    gen_max, init = par[:, 0:1], par[:, 3:4]
    cap = own_units(state_m[1], state_o[1], core)
    gen1[...] = own_units(state_m[0], state_o[0], core)
    flow[...] = by_core(flow_m[...].T, flow_s[...].T, core)
    half = dual.shape[1] // 2
    dual[...] = by_core(keep[0:half].T, other[0:half].T, core)
    own = balance.shape[1]
    first = (2 * lax.axis_index("chip") + core) * own
    side = first // half
    row = jnp.where(core == side, keep[half:half + 1], other[half:half + 1])
    wide = row.shape[1]
    row = pltpu.roll(row, lax.rem(wide - (first - side * half), wide), 1)
    balance[...] = row[:, :own]
    cap1[...] = cap
    c1, grad, start, window = (hold[i] for i in range(4))
    lanes = lax.broadcasted_iota(jnp.int32, c1.shape, 1)
    c2 = jnp.clip(c1 - TAU * (grad - gen_max * cap), 0.0, 1.0)
    bc2 = 2.0 * c2 - c1
    before = jnp.where(lanes == 0, init, pltpu.roll(bc2, 1, 1))
    commit_out[...] = c2
    bar_commit[...] = bc2
    start_out[...] = jnp.maximum(0.0, start + SIGMA * (bc2 - before))
    window_out[...] = jnp.maximum(0.0, window - SIGMA * bc2)


def units_kernel(par, gen_m, gen_o, gen1, cap1, bar_commit, gen_out, cap_out):
    g2 = own_units(gen_m[...], gen_o[...], lax.axis_index("core"))
    gen_out[...] = g2
    bar = 2.0 * g2 - gen1[...]
    cap_out[...] = jnp.maximum(0.0, cap1[...] + SIGMA * (bar - par[:, 0:1] * bar_commit[...]))


def load_kernel(ptdf, load, keep, send, demand, flow):
    step = pl.program_id(0)
    block = load[...]
    part = jnp.dot(ptdf[...], block, preferred_element_type=F32)
    rows = jnp.sum(block.astype(F32).reshape(-1, 8, block.shape[1]), axis=0)

    @pl.when(step == 0)
    def _():
        flow[...] = part
        demand[...] = rows

    @pl.when(step > 0)
    def _():
        flow[...] += part
        demand[...] += rows

    @pl.when(step == pl.num_programs(0) - 1)
    def _():
        turned = flow[...].T
        core = lax.axis_index("core")
        keep[...] = half_of(turned, core)
        send[...] = half_of(turned, 1 - core)


def slab_kernel(ptdf, *refs):
    pieces, (keep, send, demand, slab, buffers, sems) = refs[:-6], refs[-6:]
    count = buffers.shape[0]
    core, chip = lax.axis_index("core"), lax.axis_index("chip")
    side, here = chip % 2, chip // 2
    depth = slab.shape[0]
    copies = []
    for i in range(count):
        start = pl.multiple_of(jnp.bitwise_xor(here, i) * depth, depth)
        copies.append(
            pltpu.make_async_copy(ptdf.at[:, pl.ds(start, depth)], buffers.at[i], sems.at[i])
        )
        copies[i].start()
    flow, rows = 0.0, 0.0
    for i in range(count):
        near, across, swapped, far = (ref[...] for ref in pieces[4 * i:4 * i + 4])
        bus_dev, periods = near.shape
        for yy in range(2):
            for kk in range(2):
                chosen = jnp.where(
                    side == yy,
                    jnp.where(core == kk, near, swapped),
                    jnp.where(core == kk, across, far),
                )
                at = (2 * yy + kk) * bus_dev
                slab[at:at + bus_dev] = chosen
                rows += jnp.sum(chosen.astype(F32).reshape(-1, 8, periods), axis=0)
        copies[i].wait()
        flow += jnp.dot(buffers[i], slab[...], preferred_element_type=F32)
    turned = flow.T
    keep[...] = half_of(turned, core)
    send[...] = half_of(turned, 1 - core)
    demand[...] = rows


def line_step(flows, dual, bound):
    shifted = dual + SIGMA * flows
    return shifted - SIGMA * jnp.clip(shifted / SIGMA, -bound, bound)


def balance_change(bar, demand, units):
    totals = jnp.sum(bar.astype(F32), axis=1, keepdims=True)
    return (totals - demand) / units


TURN = (((1,), (1,)), ((), ()))


def line1_kernel(bars, cols_m, cols_o, flow_m, flow_o, dual, pack_m, pack_o, demand,
                 part, keep, send, held):
    core, chip = lax.axis_index("core"), lax.axis_index("chip")
    lines, units = cols_m.shape
    wide = bars.shape[2]
    for i in range(bars.shape[0]):
        held[:, i * wide:(i + 1) * wide] = bars[i]
    bar = held[...]
    mine = lax.dot_general(bar, cols_m[...], TURN, preferred_element_type=F32) - flow_m[...]
    other = lax.dot_general(bar, cols_o[...], TURN, preferred_element_type=F32) - flow_o[...]
    flows = jnp.concatenate([mine, other], axis=1)
    new = line_step(flows, dual[...], packed_limits(pack_m, pack_o, lines))
    wanted = half_of(to_column(jnp.sum(demand[...], axis=0, keepdims=True)), core)
    row = packed_row(pack_m, pack_o, 2 + lines // demand.shape[1])
    balance = half_of(to_column(row), core)
    moved = balance + balance_change(bar, wanted, units)
    periods = moved.shape[0]
    own = 2 * periods // part.shape[0]
    rows = lax.broadcasted_iota(jnp.int32, moved.shape, 0) + core * periods
    moved = jnp.where((rows >= chip * own) & (rows < (chip + 1) * own), moved, 0.0)
    put_parts(part, new, cols_m, cols_o, moved)
    row = jnp.concatenate([to_row(moved), jnp.zeros((1, lines - periods), F32)], axis=1)
    extra = jnp.broadcast_to(row, (8, lines))
    keep[0:periods] = new[:, :lines]
    keep[periods:] = extra
    send[0:periods] = new[:, lines:]
    send[periods:] = extra


def line2_kernel(bars_m, bars_o, cols, flow, dual, limit, demand, balance, dual_out, balance_out,
                 held):
    core, chip = lax.axis_index("core"), lax.axis_index("chip")
    half, wide = bars_m.shape[1:]
    for i in range(bars_m.shape[0]):
        here, there = bars_m[i], bars_o[i]
        held[0:half, i * wide:(i + 1) * wide] = jnp.where(core == 0, here, there)
        held[half:, i * wide:(i + 1) * wide] = jnp.where(core == 0, there, here)
    bar = held[...]
    flows = lax.dot_general(cols[...], bar, TURN, preferred_element_type=F32) - flow[...]
    dual_out[...] = line_step(flows, dual[...], limit[...])
    wanted = to_column(jnp.sum(demand[...], axis=0, keepdims=True))
    change = to_row(balance_change(bar, wanted, cols.shape[1]))
    own = balance_out.shape[1]
    first = (2 * chip + core) * own
    wide = change.shape[1]
    change = pltpu.roll(change, lax.rem(wide - first, wide), 1)
    balance_out[...] = balance[...] + change[:, :own]


def work(flops, moved):
    return pl.CostEstimate(flops=flops, bytes_accessed=moved, transcendentals=0)


def near_core(values):
    return pltpu.with_memory_space_constraint(values, pltpu.VMEM)


def room(mib):
    return pltpu.CompilerParams(vmem_limit_bytes=mib << 20)


def call(kernel, outs, *args, scratch=(), cost=None):
    shapes = [jax.ShapeDtypeStruct(shape, dtype) for shape, dtype in outs]
    return pl.pallas_call(
        kernel,
        out_shape=shapes,
        in_specs=[VMEM] * len(args),
        out_specs=[VMEM] * len(shapes),
        scratch_shapes=scratch,
        cost_estimate=cost,
        compiler_params=room(8),
    )(*args)


def block_depth(buses, most):
    return max(d for d in range(128, most + 1, 128) if buses % d == 0)


def swap(values):
    return lax.ppermute(values, "core", SWAP)


def gathered_product(ptdf, every_load):
    lines, buses = ptdf.shape
    periods = every_load.shape[1]
    half = periods // 2
    depth = block_depth(buses, 4608)
    return pl.pallas_call(
        load_kernel,
        grid=(buses // depth,),
        out_shape=[
            jax.ShapeDtypeStruct((half, lines), F32),
            jax.ShapeDtypeStruct((half, lines), F32),
            jax.ShapeDtypeStruct((8, periods), F32),
        ],
        in_specs=[
            pl.BlockSpec((lines, depth), lambda k: (0, k)),
            pl.BlockSpec((depth, periods), lambda k: (k, 0)),
        ],
        out_specs=[
            pl.BlockSpec((half, lines), lambda k: (0, 0)),
            pl.BlockSpec((half, lines), lambda k: (0, 0)),
            pl.BlockSpec((8, periods), lambda k: (0, 0)),
        ],
        scratch_shapes=[pltpu.VMEM((lines, periods), F32)],
        cost_estimate=work(2 * periods * lines * buses, ptdf.size * 2 + every_load.size * 2),
    )(ptdf, every_load)


def slab_product(ptdf, pieces):
    lines = ptdf.shape[0]
    bus_dev, periods = pieces[0].shape
    count, depth = len(pieces) // 4, 4 * bus_dev
    shapes = [(periods // 2, lines)] * 2 + [(8, periods)]
    moved = count * depth * (lines + periods) * 2
    return pl.pallas_call(
        slab_kernel,
        out_shape=[jax.ShapeDtypeStruct(shape, F32) for shape in shapes],
        in_specs=[HBM] + [VMEM] * len(pieces),
        out_specs=[VMEM] * len(shapes),
        scratch_shapes=[
            pltpu.VMEM((depth, periods), BF16),
            pltpu.VMEM((count, lines, depth), BF16),
            pltpu.SemaphoreType.DMA((count,)),
        ],
        cost_estimate=work(2 * lines * periods * count * depth, moved),
        compiler_params=room(16),
    )(ptdf, *pieces)


def unit_columns(ptdf, unit_bus):
    lines, buses = ptdf.shape
    units = unit_bus.shape[0]
    depth = block_depth(buses, 2304)
    return pl.pallas_call(
        columns_kernel,
        grid=(buses // depth,),
        out_shape=jax.ShapeDtypeStruct((lines, units), BF16),
        in_specs=[
            pl.BlockSpec((1, units), lambda k: (0, 0)),
            pl.BlockSpec((lines, depth), lambda k: (0, k)),
        ],
        out_specs=pl.BlockSpec((lines, units), lambda k: (0, 0)),
        scratch_shapes=[pltpu.VMEM((lines, units), F32)],
        cost_estimate=work(2 * units * lines * buses, ptdf.size * 2),
        compiler_params=room(24),
    )(unit_bus[None], ptdf)


def on_device(
    ptdf, load, unit_bus, min_up, gen_max, cost_gen, cost_commit, cost_start, init_commit,
    line_limit, gen, commit, startup, line_dual, balance_dual, cap_dual, start_dual, window_dual,
):
    unit_dev, periods = gen.shape
    lines, _ = ptdf.shape
    units = unit_bus.shape[0]
    chips = lax.axis_size("chip")
    half = periods // 2
    unit_chip = 2 * unit_dev
    across = [(i, i ^ 1) for i in range(chips)]
    by_slab = chips == 8 and 4 * load.shape[0] % 128 == 0
    after = lax.optimization_barrier

    def along(turn, piece):
        pairs = [(i, i ^ 2 * turn) for i in range(chips)]
        return lax.ppermute(piece, "chip", pairs)

    def cross(piece):
        return lax.ppermute(piece, "chip", across)

    if by_slab:
        near = [load, along(1, load), along(2, load)]
        far = [cross(load)]
    else:
        every_load = lax.all_gather(load, LINE, axis=0, tiled=True)
    dual_o, balance_o = swap(line_dual), swap(balance_dual)
    ptdf = pltpu.with_memory_space_constraint(ptdf, pltpu.HBM)

    cols_m = unit_columns(ptdf, unit_bus)
    if by_slab:
        late_load, near[1], near[2] = after((load, near[1], near[2], cols_m))[:3]
        near.append(along(3, late_load))
        far.append(cross(near[1]))
        far.append(cross(near[2]))
    cols_o = swap(cols_m)

    blocks = (chips, half, unit_chip)
    parts, dual0 = call(
        adjoint_kernel, [(blocks, F32), ((half, 2 * lines), F32)],
        cols_m, cols_o, line_dual, dual_o, balance_dual[None], balance_o[None],
    )
    commit, startup, gen_max, min_up, parts = after((commit, startup, gen_max, min_up, parts))
    sums = lax.all_to_all(parts, "chip", 0, 0)
    if by_slab:
        near[3] = after((near[3], parts))[0]
        far.append(cross(near[3]))
    par = jnp.stack(
        [gen_max, cost_commit, cost_start, init_commit, min_up.astype(F32)], axis=1
    )
    square = (unit_dev, periods)
    states = [
        pltpu.with_memory_space_constraint(state, pltpu.HBM)
        for state in (gen, commit, startup, cap_dual, start_dual, window_dual)
    ]
    pack_m, startup2, hold = call(
        ahead_kernel,
        [((3 * unit_dev + 8, periods), F32), (square, F32), ((4, *square), F32)], par,
        gen_max[None], cost_gen[None], line_limit[None], balance_dual[None], *states,
    )
    pack_o = swap(pack_m)
    spread, state_m = call(
        gen1_kernel, [(blocks, BF16), ((2, half, unit_chip), F32)], sums, pack_m, pack_o,
    )

    bars = lax.all_to_all(spread, "chip", 0, 0)
    if by_slab:
        far[3] = after((far[3], spread))[0]
        near_o = [swap(piece) for piece in near]
        far_o = [swap(piece) for piece in far[:3]]
        far_o.append(swap(far[3]))
        near_o, far_o = ([near_core(piece) for piece in some] for some in (near_o, far_o))
        pieces = [list(four) for four in zip(near, far, near_o, far_o)]
        flow_m, flow_s, demand = slab_product(ptdf, sum(pieces, []))
    else:
        flow_m, flow_s, demand = gathered_product(ptdf, every_load)
    flow_o = swap(flow_s)

    parts, keep, send = call(
        line1_kernel, [(blocks, F32)] + [((half + 8, lines), F32)] * 2,
        bars, cols_m, cols_o, flow_m, flow_o, near_core(dual0), pack_m, pack_o, demand,
        scratch=[pltpu.VMEM((half, units), BF16)],
    )
    sums = lax.all_to_all(parts, "chip", 0, 0)
    state, par, line_limit, parts = after((state_m, par, line_limit, parts))
    limit = line_limit[:, None]
    small = ((1, balance_dual.shape[0]), F32)
    state_o, dual_o = swap(state), swap(send)
    flow, gen1, cap1, bar_commit2, dual1, balance1, commit2, start2, window2 = call(
        late_kernel,
        [((lines, periods), F32)] + [(square, F32)] * 3 + [((lines, periods), F32), small]
        + [(square, F32)] * 3,
        par, state, state_o, keep, dual_o, hold, flow_m, flow_s,
    )
    state_m, bar_commit2, limit = after((state_m, bar_commit2, limit))
    spread, gen2_m = call(
        gen2_kernel, [(blocks, BF16), ((half, unit_chip), F32)], sums, state_m, pack_m, pack_o,
    )
    bars = lax.all_to_all(spread, "chip", 0, 0)
    gen2_o = swap(gen2_m)
    gen2, cap2 = call(
        units_kernel, [(square, F32)] * 2, par, gen2_m, gen2_o, gen1, cap1, bar_commit2
    )
    dual1, cap2 = after((dual1, cap2))
    dual2, balance2 = call(
        line2_kernel, [((lines, periods), F32), small],
        bars, swap(bars), cols_m, near_core(flow), dual1, limit, demand, balance1,
        scratch=[pltpu.VMEM((periods, units), BF16)],
    )
    return (gen2, commit2, startup2, dual2, balance2[0], cap2, start2, window2)


def solution(mesh):
    groups, lines = mesh.devices.shape
    mesh = Mesh(mesh.devices.reshape(groups, lines // 2, 2), ("grp", *LINE))
    wide = P(LINE, "grp")
    unit = P(LINE)
    both = P(("grp", *LINE))
    in_specs = (
        P(LINE, None), wide, P(), unit, unit, unit, unit, unit, unit, unit,
        wide, wide, wide, wide, both, wide, wide, wide,
    )
    out_specs = (wide, wide, wide, wide, both, wide, wide, wide)

    return jax.shard_map(
        on_device, mesh=mesh, in_specs=in_specs, out_specs=out_specs, check_vma=False
    )
```

```python
import jax
import jax.numpy as jnp
from jax import lax
from jax.experimental import pallas as pl
from jax.experimental.pallas import tpu as pltpu
from jax.sharding import Mesh, PartitionSpec as P

TAU = 0.05
SIGMA = 0.5
SPAN_BITS = 5

F32 = jnp.float32
BF16 = jnp.bfloat16
LINE = ("chip", "core")
SWAP = [(0, 1), (1, 0)]
VMEM = pl.BlockSpec(memory_space=pltpu.VMEM)
HBM = pl.BlockSpec(memory_space=pltpu.HBM)


def shift_right(values, amount):
    lanes = lax.broadcasted_iota(jnp.int32, values.shape, 1)
    return jnp.where(lanes >= amount, pltpu.roll(values, amount, 1), 0.0)


def shift_left(values, amount):
    periods = values.shape[1]
    lanes = lax.broadcasted_iota(jnp.int32, values.shape, 1)
    return jnp.where(lanes < periods - amount, pltpu.roll(values, periods - amount, 1), 0.0)


def window_sum(values, spans, shift):
    block = values
    total = jnp.zeros_like(values)
    for bit in range(SPAN_BITS):
        chosen = (lax.shift_right_logical(spans, bit) & 1) == 1
        total = jnp.where(chosen, block + shift(total, 1 << bit), total)
        if bit + 1 < SPAN_BITS:
            block = block + shift(block, 1 << bit)
    return total


def diagonal(rows, columns):
    shape = (rows, columns)
    return lax.broadcasted_iota(jnp.int32, shape, 0) == lax.broadcasted_iota(jnp.int32, shape, 1)


def to_column(row):
    size = row.shape[1]
    return jnp.sum(jnp.where(diagonal(size, size), row, 0.0), axis=1, keepdims=True)


def to_row(column):
    size = column.shape[0]
    return jnp.sum(jnp.where(diagonal(size, size), column, 0.0), axis=0, keepdims=True)


def half_of(values, core):
    half = values.shape[0] // 2
    return jnp.where(core == 0, values[:half], values[half:])


def by_core(mine, other, core):
    return jnp.where(
        core == 0,
        jnp.concatenate([mine, other], axis=1),
        jnp.concatenate([other, mine], axis=1),
    )


def packed_row(mine, other, index):
    at = mine.shape[0] - 8 + index
    return mine[at:at + 1] + other[at:at + 1]


def packed_limits(mine, other, lines):
    rows = []
    for pack in (mine, other):
        for i in range(lines // pack.shape[1]):
            at = pack.shape[0] - 6 + i
            rows.append(pack[at:at + 1])
    return jnp.concatenate(rows, axis=1)


def ahead_kernel(par, gen_row, cost_row, limit, balance, gen, commit, startup, cap, start, window,
                 pack, startup2, hold):
    gen_max, cost_commit, cost_start, init = (par[:, i:i + 1] for i in range(4))
    spans = jnp.broadcast_to(par[:, 4:5].astype(jnp.int32), commit.shape)
    lanes = lax.broadcasted_iota(jnp.int32, commit.shape, 1)
    c0, s0, sd0, wd0 = commit[...], startup[...], start[...], window[...]
    grad_c = cost_commit - gen_max * cap[...] + sd0 - shift_left(sd0, 1) - wd0
    grad_s = cost_start - sd0 + window_sum(wd0, spans, shift_left)
    c1 = jnp.clip(c0 - TAU * grad_c, 0.0, 1.0)
    s1 = jnp.clip(s0 - TAU * grad_s, 0.0, 1.0)
    bc1 = 2.0 * c1 - c0
    bs1 = 2.0 * s1 - s0
    before = jnp.where(lanes == 0, init, pltpu.roll(bc1, 1, 1))
    sd1 = jnp.maximum(0.0, sd0 + SIGMA * (bc1 - before - bs1))
    wd1 = jnp.maximum(0.0, wd0 + SIGMA * (window_sum(bs1, spans, shift_right) - bc1))
    grad_s2 = cost_start - sd1 + window_sum(wd1, spans, shift_left)
    s2 = jnp.clip(s1 - TAU * grad_s2, 0.0, 1.0)
    bs2 = 2.0 * s2 - s1
    units = gen.shape[0]
    pack[0:units] = gen[...]
    pack[units:2 * units] = cap[...]
    pack[2 * units:3 * units] = bc1
    core, wide = lax.axis_index("core"), pack.shape[1]
    blank = jnp.zeros((1, wide - units), F32)
    table = [pltpu.roll(jnp.concatenate([row[...], blank], axis=1), core * units, 1)
             for row in (gen_row, cost_row)]
    table += [limit[:, i:i + wide] for i in range(0, limit.shape[1], wide)]
    own = balance.shape[1]
    row = jnp.concatenate([balance[...], jnp.zeros((1, wide - own), F32)], axis=1)
    table.append(pltpu.roll(row, (2 * lax.axis_index("chip") + core) * own, 1))
    table += [jnp.zeros((1, wide), F32)] * (8 - len(table))
    pack[3 * units:] = jnp.concatenate(table, axis=0)
    startup2[...] = s2
    hold[0] = c1
    hold[1] = cost_commit + sd1 - shift_left(sd1, 1) - wd1
    hold[2] = sd1 - SIGMA * bs2
    hold[3] = wd1 + SIGMA * window_sum(bs2, spans, shift_right)


def columns_kernel(bus, ptdf, cols, acc):
    step = pl.program_id(0)
    depth = ptdf.shape[1]
    here = bus[...] - step * depth
    places = lax.broadcasted_iota(jnp.int32, (depth, bus.shape[1]), 0)
    hot = jnp.where(places == here, 1.0, 0.0).astype(BF16)
    part = jnp.dot(ptdf[...], hot, preferred_element_type=F32)

    @pl.when(step == 0)
    def _():
        acc[...] = part

    @pl.when(step > 0)
    def _():
        acc[...] += part

    @pl.when(step == pl.num_programs(0) - 1)
    def _():
        cols[...] = acc[...].astype(BF16)


def put_parts(part, dual, cols_m, cols_o, balance):
    lines = cols_m.shape[0]
    half = dual.astype(BF16)
    total = jnp.dot(half[:, :lines], cols_m[...], preferred_element_type=F32)
    total += jnp.dot(half[:, lines:], cols_o[...], preferred_element_type=F32)
    total += balance
    wide = part.shape[2]
    for i in range(part.shape[0]):
        part[i] = total[:, i * wide:(i + 1) * wide]


def balance_column(mine, other, periods):
    core, chip = lax.axis_index("core"), lax.axis_index("chip")
    own = mine.shape[1]
    rest = jnp.zeros((1, periods - 2 * own), F32)
    row = jnp.concatenate([by_core(mine[...], other[...], core), rest], axis=1)
    return half_of(to_column(pltpu.roll(row, 2 * chip * own, 1)), core)


def adjoint_kernel(cols_m, cols_o, dual_m, dual_o, balance_m, balance_o, part, dual_t):
    core = lax.axis_index("core")
    dual = jnp.concatenate([half_of(dual_m[...].T, core), half_of(dual_o[...].T, core)], axis=1)
    dual_t[...] = dual
    column = balance_column(balance_m, balance_o, dual_m.shape[1])
    put_parts(part, dual, cols_m, cols_o, column)


def gen_step(parts, gen, cap, pack_m, pack_o):
    weighted = parts[0]
    for i in range(1, parts.shape[0]):
        weighted = weighted + parts[i]
    gen_max = packed_row(pack_m, pack_o, 0)
    cost_gen = packed_row(pack_m, pack_o, 1)
    g1 = jnp.clip(gen - TAU * (cost_gen + (weighted + cap)), 0.0, gen_max)
    return g1, 2.0 * g1 - gen, gen_max


def gen1_kernel(parts, pack_m, pack_o, spread, state):
    core = lax.axis_index("core")
    units = (pack_m.shape[0] - 8) // 3

    def turned(i):
        rows = slice(i * units, (i + 1) * units)
        return by_core(half_of(pack_m[rows].T, core), half_of(pack_o[rows].T, core), core)

    cap = turned(1)
    g1, bar, gen_max = gen_step(parts, turned(0), cap, pack_m, pack_o)
    half = bar.astype(BF16)
    for i in range(spread.shape[0]):
        spread[i] = half
    state[0] = g1
    state[1] = jnp.maximum(0.0, cap + SIGMA * (bar - gen_max * turned(2)))


def gen2_kernel(parts, state, pack_m, pack_o, spread, gen_out):
    g2, bar, _ = gen_step(parts, state[0], state[1], pack_m, pack_o)
    half = bar.astype(BF16)
    for i in range(spread.shape[0]):
        spread[i] = half
    gen_out[...] = g2


def own_units(mine, other, core):
    units = mine.shape[1] // 2
    here, there = mine.T, other.T
    here = jnp.where(core == 0, here[:units], here[units:])
    there = jnp.where(core == 0, there[:units], there[units:])
    return by_core(here, there, core)


def late_kernel(par, state_m, state_o, keep, other, hold, flow_m, flow_s,
                flow, gen1, cap1, bar_commit, dual, balance, commit_out, start_out, window_out):
    core = lax.axis_index("core")
    gen_max, init = par[:, 0:1], par[:, 3:4]
    cap = own_units(state_m[1], state_o[1], core)
    gen1[...] = own_units(state_m[0], state_o[0], core)
    flow[...] = by_core(flow_m[...].T, flow_s[...].T, core)
    half = dual.shape[1] // 2
    dual[...] = by_core(keep[0:half].T, other[0:half].T, core)
    own = balance.shape[1]
    first = (2 * lax.axis_index("chip") + core) * own
    side = first // half
    row = jnp.where(core == side, keep[half:half + 1], other[half:half + 1])
    wide = row.shape[1]
    row = pltpu.roll(row, lax.rem(wide - (first - side * half), wide), 1)
    balance[...] = row[:, :own]
    cap1[...] = cap
    c1, grad, start, window = (hold[i] for i in range(4))
    lanes = lax.broadcasted_iota(jnp.int32, c1.shape, 1)
    c2 = jnp.clip(c1 - TAU * (grad - gen_max * cap), 0.0, 1.0)
    bc2 = 2.0 * c2 - c1
    before = jnp.where(lanes == 0, init, pltpu.roll(bc2, 1, 1))
    commit_out[...] = c2
    bar_commit[...] = bc2
    start_out[...] = jnp.maximum(0.0, start + SIGMA * (bc2 - before))
    window_out[...] = jnp.maximum(0.0, window - SIGMA * bc2)


def units_kernel(par, gen_m, gen_o, gen1, cap1, bar_commit, gen_out, cap_out):
    g2 = own_units(gen_m[...], gen_o[...], lax.axis_index("core"))
    gen_out[...] = g2
    bar = 2.0 * g2 - gen1[...]
    cap_out[...] = jnp.maximum(0.0, cap1[...] + SIGMA * (bar - par[:, 0:1] * bar_commit[...]))


def load_kernel(ptdf, load, keep, send, demand, flow):
    step = pl.program_id(0)
    block = load[...]
    part = jnp.dot(ptdf[...], block, preferred_element_type=F32)
    rows = jnp.sum(block.astype(F32).reshape(-1, 8, block.shape[1]), axis=0)

    @pl.when(step == 0)
    def _():
        flow[...] = part
        demand[...] = rows

    @pl.when(step > 0)
    def _():
        flow[...] += part
        demand[...] += rows

    @pl.when(step == pl.num_programs(0) - 1)
    def _():
        turned = flow[...].T
        core = lax.axis_index("core")
        keep[...] = half_of(turned, core)
        send[...] = half_of(turned, 1 - core)


def slab_kernel(ptdf, *refs):
    pieces, (keep, send, demand, slab, buffers, sems) = refs[:-6], refs[-6:]
    count = buffers.shape[0]
    core, chip = lax.axis_index("core"), lax.axis_index("chip")
    side, here = chip % 2, chip // 2
    depth = slab.shape[1]
    copies = []
    for i in range(count):
        start = pl.multiple_of(jnp.bitwise_xor(here, i) * depth, depth)
        copies.append(
            pltpu.make_async_copy(ptdf.at[:, pl.ds(start, depth)], buffers.at[i], sems.at[i])
        )
        copies[i].start()
    rows = 0.0
    for i in range(count):
        near, across, swapped, far = (ref[...] for ref in pieces[4 * i:4 * i + 4])
        bus_dev, periods = near.shape
        for yy in range(2):
            for kk in range(2):
                chosen = jnp.where(
                    side == yy,
                    jnp.where(core == kk, near, swapped),
                    jnp.where(core == kk, across, far),
                )
                at = (2 * yy + kk) * bus_dev
                slab[i, at:at + bus_dev] = chosen
                rows += jnp.sum(chosen.astype(F32).reshape(-1, 8, periods), axis=0)
    flow = 0.0
    for i in range(count):
        copies[i].wait()
        flow += jnp.dot(buffers[i], slab[i], preferred_element_type=F32)
    turned = flow.T
    keep[...] = half_of(turned, core)
    send[...] = half_of(turned, 1 - core)
    demand[...] = rows


def line_step(flows, dual, bound):
    shifted = dual + SIGMA * flows
    return shifted - SIGMA * jnp.clip(shifted / SIGMA, -bound, bound)


def balance_change(bar, demand, units):
    totals = jnp.sum(bar.astype(F32), axis=1, keepdims=True)
    return (totals - demand) / units


TURN = (((1,), (1,)), ((), ()))


def line1_kernel(bars, cols_m, cols_o, flow_m, flow_o, dual, pack_m, pack_o, demand,
                 part, keep, send, held):
    core, chip = lax.axis_index("core"), lax.axis_index("chip")
    lines, units = cols_m.shape
    wide = bars.shape[2]
    for i in range(bars.shape[0]):
        held[:, i * wide:(i + 1) * wide] = bars[i]
    bar = held[...]
    mine = lax.dot_general(bar, cols_m[...], TURN, preferred_element_type=F32) - flow_m[...]
    other = lax.dot_general(bar, cols_o[...], TURN, preferred_element_type=F32) - flow_o[...]
    flows = jnp.concatenate([mine, other], axis=1)
    new = line_step(flows, dual[...], packed_limits(pack_m, pack_o, lines))
    wanted = half_of(to_column(jnp.sum(demand[...], axis=0, keepdims=True)), core)
    row = packed_row(pack_m, pack_o, 2 + lines // demand.shape[1])
    balance = half_of(to_column(row), core)
    moved = balance + balance_change(bar, wanted, units)
    periods = moved.shape[0]
    own = 2 * periods // part.shape[0]
    rows = lax.broadcasted_iota(jnp.int32, moved.shape, 0) + core * periods
    moved = jnp.where((rows >= chip * own) & (rows < (chip + 1) * own), moved, 0.0)
    put_parts(part, new, cols_m, cols_o, moved)
    row = jnp.concatenate([to_row(moved), jnp.zeros((1, lines - periods), F32)], axis=1)
    extra = jnp.broadcast_to(row, (8, lines))
    keep[0:periods] = new[:, :lines]
    keep[periods:] = extra
    send[0:periods] = new[:, lines:]
    send[periods:] = extra


def line2_kernel(bars_m, bars_o, cols, flow, dual, limit, demand, balance, dual_out, balance_out,
                 held):
    core, chip = lax.axis_index("core"), lax.axis_index("chip")
    half, wide = bars_m.shape[1:]
    for i in range(bars_m.shape[0]):
        here, there = bars_m[i], bars_o[i]
        held[0:half, i * wide:(i + 1) * wide] = jnp.where(core == 0, here, there)
        held[half:, i * wide:(i + 1) * wide] = jnp.where(core == 0, there, here)
    bar = held[...]
    flows = lax.dot_general(cols[...], bar, TURN, preferred_element_type=F32) - flow[...]
    dual_out[...] = line_step(flows, dual[...], limit[...])
    wanted = to_column(jnp.sum(demand[...], axis=0, keepdims=True))
    change = to_row(balance_change(bar, wanted, cols.shape[1]))
    own = balance_out.shape[1]
    first = (2 * chip + core) * own
    wide = change.shape[1]
    change = pltpu.roll(change, lax.rem(wide - first, wide), 1)
    balance_out[...] = balance[...] + change[:, :own]


def work(flops, moved):
    return pl.CostEstimate(flops=flops, bytes_accessed=moved, transcendentals=0)


def near_core(values):
    return pltpu.with_memory_space_constraint(values, pltpu.VMEM)


def room(mib):
    return pltpu.CompilerParams(vmem_limit_bytes=mib << 20)


def call(kernel, outs, *args, scratch=(), cost=None):
    shapes = [pltpu.HBM(shape, dtype) if dtype == BF16 else jax.ShapeDtypeStruct(shape, dtype) for shape, dtype in outs]
    return pl.pallas_call(
        kernel,
        out_shape=shapes,
        in_specs=[VMEM] * len(args),
        out_specs=[VMEM] * len(shapes),
        scratch_shapes=scratch,
        cost_estimate=cost,
        compiler_params=room(8),
    )(*args)


def block_depth(buses, most):
    return max(d for d in range(128, most + 1, 128) if buses % d == 0)


def swap(values):
    return lax.ppermute(values, "core", SWAP)


def gathered_product(ptdf, every_load):
    lines, buses = ptdf.shape
    periods = every_load.shape[1]
    half = periods // 2
    depth = block_depth(buses, 4608)
    return pl.pallas_call(
        load_kernel,
        grid=(buses // depth,),
        out_shape=[
            jax.ShapeDtypeStruct((half, lines), F32),
            jax.ShapeDtypeStruct((half, lines), F32),
            jax.ShapeDtypeStruct((8, periods), F32),
        ],
        in_specs=[
            pl.BlockSpec((lines, depth), lambda k: (0, k)),
            pl.BlockSpec((depth, periods), lambda k: (k, 0)),
        ],
        out_specs=[
            pl.BlockSpec((half, lines), lambda k: (0, 0)),
            pl.BlockSpec((half, lines), lambda k: (0, 0)),
            pl.BlockSpec((8, periods), lambda k: (0, 0)),
        ],
        scratch_shapes=[pltpu.VMEM((lines, periods), F32)],
        cost_estimate=work(2 * periods * lines * buses, ptdf.size * 2 + every_load.size * 2),
    )(ptdf, every_load)


def slab_product(ptdf, pieces):
    lines = ptdf.shape[0]
    bus_dev, periods = pieces[0].shape
    count, depth = len(pieces) // 4, 4 * bus_dev
    shapes = [(periods // 2, lines)] * 2 + [(8, periods)]
    moved = count * depth * (lines + periods) * 2
    return pl.pallas_call(
        slab_kernel,
        out_shape=[jax.ShapeDtypeStruct(shape, F32) for shape in shapes],
        in_specs=[HBM] + [VMEM] * len(pieces),
        out_specs=[VMEM] * len(shapes),
        scratch_shapes=[
            pltpu.VMEM((count, depth, periods), BF16),
            pltpu.VMEM((count, lines, depth), BF16),
            pltpu.SemaphoreType.DMA((count,)),
        ],
        cost_estimate=work(2 * lines * periods * count * depth, moved),
        compiler_params=room(20),
    )(ptdf, *pieces)


def unit_columns(ptdf, unit_bus):
    lines, buses = ptdf.shape
    units = unit_bus.shape[0]
    depth = block_depth(buses, 4608)
    return pl.pallas_call(
        columns_kernel,
        grid=(buses // depth,),
        out_shape=jax.ShapeDtypeStruct((lines, units), BF16),
        in_specs=[
            pl.BlockSpec((1, units), lambda k: (0, 0)),
            pl.BlockSpec((lines, depth), lambda k: (0, k)),
        ],
        out_specs=pl.BlockSpec((lines, units), lambda k: (0, 0)),
        scratch_shapes=[pltpu.VMEM((lines, units), F32)],
        cost_estimate=work(2 * units * lines * buses, ptdf.size * 2),
        compiler_params=room(36),
    )(pltpu.with_memory_space_constraint(unit_bus[None], pltpu.HBM), ptdf)


def on_device(
    ptdf, load, unit_bus, min_up, gen_max, cost_gen, cost_commit, cost_start, init_commit,
    line_limit, gen, commit, startup, line_dual, balance_dual, cap_dual, start_dual, window_dual,
):
    unit_dev, periods = gen.shape
    lines, _ = ptdf.shape
    units = unit_bus.shape[0]
    chips = lax.axis_size("chip")
    half = periods // 2
    unit_chip = 2 * unit_dev
    across = [(i, i ^ 1) for i in range(chips)]
    by_slab = chips == 8 and 4 * load.shape[0] % 128 == 0
    after = lax.optimization_barrier

    def along(turn, piece):
        pairs = [(i, i ^ 2 * turn) for i in range(chips)]
        return lax.ppermute(piece, "chip", pairs)

    def cross(piece):
        return lax.ppermute(piece, "chip", across)

    if by_slab:
        near = [load, along(1, load), along(2, load)]
        far = [cross(load)]
    else:
        every_load = lax.all_gather(load, LINE, axis=0, tiled=True)
    dual_o, balance_o = swap(line_dual), swap(balance_dual)
    ptdf = pltpu.with_memory_space_constraint(ptdf, pltpu.HBM)

    cols_m = unit_columns(ptdf, unit_bus)
    if by_slab:
        late_load, near[1], near[2] = after((load, near[1], near[2], cols_m))[:3]
        near.append(along(3, late_load))
        far.append(cross(near[1]))
        far.append(cross(near[2]))
    cols_o = swap(cols_m)

    blocks = (chips, half, unit_chip)
    parts, dual0 = call(
        adjoint_kernel, [(blocks, F32), ((half, 2 * lines), F32)],
        cols_m, cols_o, line_dual, dual_o, balance_dual[None], balance_o[None],
    )
    commit, startup, gen_max, min_up, parts = after((commit, startup, gen_max, min_up, parts))
    sums = lax.all_to_all(parts, "chip", 0, 0)
    if by_slab:
        near[3] = after((near[3], parts))[0]
        far.append(cross(near[3]))
    par = jnp.stack(
        [gen_max, cost_commit, cost_start, init_commit, min_up.astype(F32)], axis=1
    )
    square = (unit_dev, periods)
    states = [
        pltpu.with_memory_space_constraint(state, pltpu.HBM)
        for state in (gen, commit, startup, cap_dual, start_dual, window_dual)
    ]
    pack_m, startup2, hold = call(
        ahead_kernel,
        [((3 * unit_dev + 8, periods), F32), (square, F32), ((4, *square), F32)], par,
        gen_max[None], cost_gen[None], line_limit[None], balance_dual[None], *states,
    )
    pack_o = swap(pack_m)
    spread, state_m = call(
        gen1_kernel, [(blocks, BF16), ((2, half, unit_chip), F32)], sums, pack_m, pack_o,
    )

    bars = lax.all_to_all(spread, "chip", 0, 0)
    if by_slab:
        far[3] = after((far[3], spread))[0]
        near_o = [swap(piece) for piece in near]
        far_o = [swap(piece) for piece in far[:3]]
        far_o.append(swap(far[3]))
        near_o, far_o = ([near_core(piece) for piece in some] for some in (near_o, far_o))
        pieces = [list(four) for four in zip(near, far, near_o, far_o)]
        flow_m, flow_s, demand = slab_product(ptdf, sum(pieces, []))
    else:
        flow_m, flow_s, demand = gathered_product(ptdf, every_load)
    flow_o = swap(flow_s)

    parts, keep, send = call(
        line1_kernel, [(blocks, F32)] + [((half + 8, lines), F32)] * 2,
        bars, cols_m, cols_o, flow_m, flow_o, near_core(dual0), pack_m, pack_o, demand,
        scratch=[pltpu.VMEM((half, units), BF16)],
    )
    sums = lax.all_to_all(parts, "chip", 0, 0)
    state, par, line_limit, parts = after((state_m, par, line_limit, parts))
    limit = line_limit[:, None]
    small = ((1, balance_dual.shape[0]), F32)
    state_o, dual_o = swap(state), swap(send)
    flow, gen1, cap1, bar_commit2, dual1, balance1, commit2, start2, window2 = call(
        late_kernel,
        [((lines, periods), F32)] + [(square, F32)] * 3 + [((lines, periods), F32), small]
        + [(square, F32)] * 3,
        par, state, state_o, keep, dual_o, hold, flow_m, flow_s,
    )
    state_m, bar_commit2, limit = after((state_m, bar_commit2, limit))
    spread, gen2_m = call(
        gen2_kernel, [(blocks, BF16), ((half, unit_chip), F32)], sums, state_m, pack_m, pack_o,
    )
    bars = lax.all_to_all(spread, "chip", 0, 0)
    gen2_o = swap(gen2_m)
    gen2, cap2 = call(
        units_kernel, [(square, F32)] * 2, par, gen2_m, gen2_o, gen1, cap1, bar_commit2
    )
    dual1, cap2 = after((dual1, cap2))
    dual2, balance2 = call(
        line2_kernel, [((lines, periods), F32), small],
        bars, swap(bars), cols_m, near_core(flow), dual1, limit, demand, balance1,
        scratch=[pltpu.VMEM((periods, units), BF16)],
    )
    return (gen2, commit2, startup2, dual2, balance2[0], cap2, start2, window2)


def solution(mesh):
    groups, lines = mesh.devices.shape
    mesh = Mesh(mesh.devices.reshape(groups, lines // 2, 2), ("grp", *LINE))
    wide = P(LINE, "grp")
    unit = P(LINE)
    both = P(("grp", *LINE))
    in_specs = (
        P(LINE, None), wide, P(), unit, unit, unit, unit, unit, unit, unit,
        wide, wide, wide, wide, both, wide, wide, wide,
    )
    out_specs = (wide, wide, wide, wide, both, wide, wide, wide)

    return jax.shard_map(
        on_device, mesh=mesh, in_specs=in_specs, out_specs=out_specs, check_vma=False
    )
```
